32 devices in a mesh: tm: 4 (over y, x), space: 8 (over z, core).
Axes of the slice: x: 2, y: 2, z: 4, core: 2. Of those that a mesh axis runs over, the one named last changes fastest.
Arguments:
- frames_in: bfloat16 [32, 512, 1024], P('tm', 'space'), may hold values from -6 to 6
- time_gain: float32 [1024], replicated, may hold values from 0.1 to 1.9
- time_shift: float32 [1024], replicated, may hold values from -4 to 4
- time_query: bfloat16 [1024, 1024], replicated
- time_key: bfloat16 [1024, 1024], replicated
- time_value: bfloat16 [1024, 1024], replicated, may hold values from -0.1875 to 0.1875
- time_out: bfloat16 [1024, 1024], replicated, may hold values from -0.1875 to 0.1875
- space_gain: float32 [1024], replicated, may hold values from 0.1 to 1.9
- space_shift: float32 [1024], replicated, may hold values from -4 to 4
- space_query: bfloat16 [1024, 1024], replicated
- space_key: bfloat16 [1024, 1024], replicated
- space_value: bfloat16 [1024, 1024], replicated, may hold values from -0.1875 to 0.1875
- space_out: bfloat16 [1024, 1024], replicated, may hold values from -0.1875 to 0.1875
Outputs:
- frames_out: bfloat16 [32, 512, 1024], P('tm', 'space')
The draws below stay inside these ranges and needn't reach their ends.
All inputs are finite; a program needn't handle non-finite values.
Results may differ from the reference program's by a relative error of at most 0.03.
Values may be sent and summed in bfloat16 or wider, within the bound.
A program may use at most 192 MiB of HBM per device.

```python
import math
import jax
import jax.numpy as jnp
from jax import lax

D = 1024
HEADS = 16
HEAD_DIM = 64
FRAMES = 32
PATCHES = 512


def paired(key, group, which):
    group_key = jax.random.fold_in(key, group)
    factor = (12.0 / HEAD_DIM ** 0.5) ** 0.5
    base = jnp.clip(jax.random.normal(jax.random.fold_in(group_key, which), (D, D), jnp.float32), -4.0, 4.0)
    return (base * factor * D ** (-0.5)).astype(jnp.bfloat16)


def draw_time_query(key, part):
    return paired(key, 1, 0)


def draw_time_key(key, part):
    return paired(key, 1, 1)


def draw_space_query(key, part):
    return paired(key, 2, 0)


def draw_space_key(key, part):
    return paired(key, 2, 1)


def levels(own_key, extent, split, smallest, largest):
    def one(dim, parts):
        draws = jax.random.uniform(jax.random.fold_in(jax.random.fold_in(own_key, 6), dim), (parts,), jnp.float32, smallest / len(split), largest / len(split))
        return jnp.repeat(jnp.exp(draws), extent[dim] // parts).reshape((-1,) + (1,) * (len(extent) - dim - 1))

    loudness = one(*split[0])
    for cut in split[1:]:
        loudness = loudness * one(*cut)
    return loudness


def centred(stream_key, shape, deviation, most, pieces=(), kind=jnp.bfloat16):
    values = deviation * jax.random.normal(stream_key, shape, jnp.float32)
    if pieces:
        values = values * levels(stream_key, shape, pieces, -0.22, 0.18)
    return jnp.clip(values, -most, most).astype(kind)


def setup_inputs(seed: int = 0) -> dict:
    arg_keys = jax.random.split(jax.random.key(seed), 14)
    frames_in = centred(arg_keys[0], (FRAMES, PATCHES, D), 1.0, 6.0, ((0, 4), (1, 8)))
    time_gain = jnp.clip(1.0 + 0.18 * jax.random.normal(arg_keys[1], (D,), jnp.float32), 0.1, 1.9)
    time_shift = centred(arg_keys[2], (D,), 1.0, 4.0, (), jnp.float32)
    time_query = draw_time_query(jax.random.fold_in(arg_keys[13], 71), 0)
    time_key = draw_time_key(jax.random.fold_in(arg_keys[13], 71), 0)
    time_value = centred(arg_keys[5], (D, D), D ** -0.5, 0.1875)
    time_out = centred(arg_keys[6], (D, D), D ** -0.5, 0.1875)
    space_gain = jnp.clip(1.0 + 0.18 * jax.random.normal(arg_keys[7], (D,), jnp.float32), 0.1, 1.9)
    space_shift = centred(arg_keys[8], (D,), 1.0, 4.0, (), jnp.float32)
    space_query = draw_space_query(jax.random.fold_in(arg_keys[13], 71), 0)
    space_key = draw_space_key(jax.random.fold_in(arg_keys[13], 71), 0)
    space_value = centred(arg_keys[11], (D, D), D ** -0.5, 0.1875)
    space_out = centred(arg_keys[12], (D, D), D ** -0.5, 0.1875)
    return dict(frames_in=frames_in, time_gain=time_gain, time_shift=time_shift, time_query=time_query, time_key=time_key, time_value=time_value, time_out=time_out, space_gain=space_gain, space_shift=space_shift, space_query=space_query, space_key=space_key, space_value=space_value, space_out=space_out)


def layer_norm(tokens, gain, shift):
    values = tokens.astype(jnp.float32)
    mean_value = lax.optimization_barrier(jnp.mean(values, axis=-1, keepdims=True))
    variance = lax.optimization_barrier(jnp.mean((values - mean_value) ** 2, axis=-1, keepdims=True))
    return ((values - mean_value) * lax.rsqrt(variance + 1e-05) * gain + shift).astype(jnp.bfloat16)

def project(tokens, weight):
    return jnp.dot(tokens, weight, preferred_element_type=jnp.float32)

def attend(queries, keys_in, values_in):
    scores = jnp.einsum('bqhd,bkhd->bhqk', queries.astype(jnp.float32), keys_in.astype(jnp.float32)) * 0.125
    weights = jax.nn.softmax(scores, axis=-1).astype(jnp.bfloat16)
    result = jnp.einsum('bhqk,bkhd->bqhd', weights.astype(jnp.float32), values_in.astype(jnp.float32))
    return result.astype(jnp.bfloat16)

def heads_of(tokens):
    return tokens.reshape(FRAMES, PATCHES, HEADS, HEAD_DIM)

def reference(frames_in, time_gain, time_shift, time_query, time_key, time_value, time_out, space_gain, space_shift, space_query, space_key, space_value, space_out):
    normed = layer_norm(frames_in, time_gain, time_shift)
    block_size = math.gcd(PATCHES, 64)
    groups = []
    for weight in (time_query, time_key, time_value):
        heads = heads_of(project(normed, weight).astype(jnp.bfloat16))
        heads = jnp.transpose(heads, (1, 0, 2, 3)).reshape(PATCHES // block_size, block_size, FRAMES, HEADS, HEAD_DIM)
        groups.append(heads)

    def time_block(triple):
        return attend(triple[0], triple[1], triple[2])
    attended = lax.map(time_block, tuple(groups))
    attended = jnp.transpose(attended.reshape(PATCHES, FRAMES, D), (1, 0, 2))
    after_time = (frames_in.astype(jnp.float32) + project(attended, time_out)).astype(jnp.bfloat16)
    normed = layer_norm(after_time, space_gain, space_shift)
    triple = tuple((heads_of(project(normed, weight).astype(jnp.bfloat16)) for weight in (space_query, space_key, space_value)))

    def space_frame(frame_triple):
        return attend(frame_triple[0][None], frame_triple[1][None], frame_triple[2][None])[0]
    spatial = lax.map(space_frame, triple).reshape(FRAMES, PATCHES, D)
    return (after_time.astype(jnp.float32) + project(spatial, space_out)).astype(jnp.bfloat16)
```

```python
import functools
import math

import jax
import jax.numpy as jnp
from jax import lax
from jax.experimental import pallas as pl
from jax.experimental.pallas import tpu as pltpu
from jax.sharding import PartitionSpec as P

HEAD_DIM = 64
LANES = 128
UNROLL_T, UNROLL_S = 8, 8
SCALE = 0.125 * math.log2(math.e)
F32, BF16 = jnp.float32, jnp.bfloat16


def layer_norm(tokens, gain, shift):
    values = tokens.astype(F32)
    mean_value = jnp.mean(values, axis=-1, keepdims=True)
    centred = values - mean_value
    variance = jnp.mean(centred * centred, axis=-1, keepdims=True)
    return (centred * lax.rsqrt(variance + 1e-05) * gain + shift).astype(BF16)


def project(tokens, weight):
    return jnp.dot(tokens, weight, preferred_element_type=F32)


def permutation(rows, inner, outer, back):
    row = lax.broadcasted_iota(jnp.int32, (rows, rows), 1 if back else 0)
    col = lax.broadcasted_iota(jnp.int32, (rows, rows), 0 if back else 1)
    return jnp.where((row % inner) * outer + row // inner == col, 1.0, 0.0).astype(BF16)


def lane_masks(width):
    lane = lax.broadcasted_iota(jnp.int32, (1, LANES), 1)
    return [(lane // HEAD_DIM == part) for part in range(LANES // HEAD_DIM)]


def attend(queries, keys_in, values_in, same):
    rows = queries.shape[0]
    masks = lane_masks(LANES)
    own = jnp.concatenate([jnp.where(mask, queries, jnp.zeros_like(queries)) for mask in masks], 0)
    scores = lax.dot_general(own, keys_in, (((1,), (1,)), ((), ())), preferred_element_type=F32)
    if same is not None:
        scores = jnp.where(jnp.concatenate([same] * len(masks), 0), scores, -1e30)
    top = jnp.max(scores, axis=-1, keepdims=True)
    weights = jnp.exp2((scores - top) * SCALE).astype(BF16)
    both = jnp.concatenate([values_in, jnp.ones_like(values_in)], 1)
    added = jnp.dot(weights, both, preferred_element_type=F32)
    added = added[:, :LANES] / added[:, LANES:]
    result = added[:rows]
    for part in range(1, len(masks)):
        result = jnp.where(masks[part], added[part * rows : (part + 1) * rows], result)
    return result.astype(BF16)


def qkv(normed, weights, waits, outs):
    for weight, wait, out in zip(weights, waits, outs):
        wait()
        out[...] = project(normed, weight[...]).astype(BF16)


def time_branch(frames, x, gain, shift, weights, waits, q, k, v, a):
    rows, width = q.shape
    places = rows // frames
    order = permutation(rows, frames, places, False)
    x = project(order, x).astype(BF16)
    qkv(layer_norm(x, gain, shift), weights[:3], waits[:3], (q, k, v))
    size = max(frames, LANES)
    same = (
        lax.broadcasted_iota(jnp.int32, (size, size), 0) // frames
        == lax.broadcasted_iota(jnp.int32, (size, size), 1) // frames
    )

    def pair(index, carry):
        cols = pl.ds(pl.multiple_of(index * LANES, LANES), LANES)
        for group in range(rows // size):
            part = (pl.ds(group * size, size), cols)
            a[part] = attend(q[part], k[part], v[part], same)
        return carry

    lax.fori_loop(0, width // LANES, pair, 0, unroll=UNROLL_T)
    waits[3]()
    after = (x.astype(F32) + project(a[...], weights[3][...])).astype(BF16)
    return project(permutation(rows, frames, places, True), after)


def branch_kernel(branch, x, gain, shift, w0, w1, w2, w3, out, held, q, k, v, a, sems):
    copies = [
        pltpu.make_async_copy(w, held.at[i], sems.at[i]) for i, w in enumerate((w0, w1, w2, w3))
    ]
    for copy in copies:
        copy.start()
    weights = [held.at[i] for i in range(4)]
    waits = [copy.wait for copy in copies]
    out[...] = branch(x[...], gain[...], shift[...], weights, waits, q, k, v, a).astype(BF16)


def run_branch(branch, x, gain, shift, *weights):
    rows, width = x.shape
    vmem = pl.BlockSpec(memory_space=pltpu.VMEM)
    return pl.pallas_call(
        functools.partial(branch_kernel, branch),
        out_shape=jax.ShapeDtypeStruct((rows, width), BF16),
        in_specs=[vmem] * 3 + [pl.BlockSpec(memory_space=pl.ANY)] * 4,
        out_specs=vmem,
        scratch_shapes=[pltpu.VMEM((4, width, width), BF16)]
        + [pltpu.VMEM((rows, width), BF16)] * 4
        + [pltpu.SemaphoreType.DMA((4,))],
        compiler_params=pltpu.CompilerParams(vmem_limit_bytes=60 << 20),
    )(x, gain.reshape(1, -1), shift.reshape(1, -1), *weights)


def bit_steps(index, count):
    out, bit = [], 1
    while bit < count:
        out.append((bit, bit - 2 * bit * ((index // bit) % 2)))
        bit *= 2
    return out


def moved(index, steps, mask):
    for bit, step in steps:
        if mask & bit:
            index = index + step
    return index


def layer_kernel(
    slots,
    spread,
    x,
    tg,
    ts,
    sg,
    ss,
    *refs,
):
    sources, out = refs[:8], refs[8]
    held, xt, snd, rcv, q, k, v, a, wsem, lsem, s1, r1, s2, r2, s3, r3 = refs[9:]
    me_t, me_s = lax.axis_index("tm"), lax.axis_index("space")
    frames, piece, width = xt.shape[1:]
    rows, halves = frames // slots, xt.shape[0]
    peers = slots * spread
    chips = spread // 2
    tokens = frames * piece
    me_c = me_s % 2
    me_z = me_s // 2
    steps_t, steps_s = bit_steps(me_t, slots), bit_steps(me_s, spread)
    steps_z = bit_steps(me_z, chips)

    barrier = pltpu.get_barrier_semaphore()
    for mask in range(1, peers):
        pl.semaphore_signal(
            barrier,
            inc=1,
            device_id={
                "tm": moved(me_t, steps_t, mask % slots),
                "space": moved(me_s, steps_s, mask // slots),
            },
        )
    loads = [pltpu.make_async_copy(w, held.at[i], wsem.at[i]) for i, w in enumerate(sources)]
    locals_in = [
        pltpu.make_async_copy(
            x.at[:, me_t, h], xt.at[h, pl.ds(me_t * rows, rows)], lsem.at[h]
        )
        for h in range(halves)
    ]
    for copy in locals_in + loads:
        copy.start()
    pl.semaphore_wait(barrier, peers - 1)

    def first(h, mask):
        t = moved(me_t, steps_t, mask)
        return pltpu.make_async_remote_copy(
            src_ref=x.at[:, t, h],
            dst_ref=xt.at[h, pl.ds(me_t * rows, rows)],
            send_sem=s1.at[h, mask],
            recv_sem=r1.at[h, mask],
            device_id={"tm": t},
        )

    def second(h, mask, core):
        t, z = moved(me_t, steps_t, mask % slots), moved(me_z, steps_z, mask // slots)
        return pltpu.make_async_remote_copy(
            src_ref=snd.at[h, (t * chips + z) * 2 + core],
            dst_ref=rcv.at[h * peers + me_s * slots + me_t],
            send_sem=s2.at[h, mask, core],
            recv_sem=r2.at[h, mask, me_c],
            device_id={"tm": t, "space": z * 2 + core},
        )

    def second_wait(h, mask, core):
        return pltpu.make_async_remote_copy(
            src_ref=snd.at[0, 0],
            dst_ref=rcv.at[0],
            send_sem=s2.at[h, mask, core],
            recv_sem=r2.at[h, mask, core],
            device_id={"tm": me_t, "space": me_s + 1 - 2 * me_c},
        )

    for h in range(halves):
        for mask in range(slots - 1, 0, -1):
            first(h, mask).start()

    weights = [held.at[i] for i in range(8)]
    waits = [copy.wait for copy in loads]

    def send(h, core, masks):
        for mask in masks:
            second(h, mask, core).start()

    everyone = list(range(slots * chips - 1, 0, -1))
    late = []
    for h in range(halves):
        locals_in[h].wait()
        for mask in range(1, slots):
            first(h, mask).wait_recv()
        part = [ref.at[pl.ds(0, tokens)] for ref in (q, k, v, a)]
        after = time_branch(
            frames,
            xt[h].astype(F32).reshape(tokens, width).astype(BF16),
            tg[...],
            ts[...],
            weights[:4],
            waits[:4] if h == 0 else [lambda: None] * 4,
            *part,
        )
        snd[h] = after.reshape(frames, piece, width).astype(BF16)
        send(h, 0, everyone)
        if h < halves - 1:
            late.append(h)
        else:
            for held_back in late + [h]:
                send(held_back, 1, everyone)
        other = 1 - me_c
        pltpu.make_async_remote_copy(
            src_ref=snd.at[h, (me_t * chips + me_z) * 2 + other],
            dst_ref=rcv.at[h * peers + me_s * slots + me_t],
            send_sem=s2.at[h, 0, 0],
            recv_sem=r2.at[h, 0, 0],
            device_id={"space": me_z * 2 + other},
        ).start()
        rcv[h * peers + me_s * slots + me_t] = snd[h, me_t * rows + me_s]

    for h in range(halves):
        for mask in everyone:
            for core in range(2):
                second_wait(h, mask, core).wait_recv()
        second_wait(h, 0, 0).wait_recv()
        frame = rcv[pl.ds(h * peers, peers)].astype(F32).reshape(tokens, width).astype(BF16)
        qkv(
            layer_norm(frame, sg[...], ss[...]),
            weights[4:7],
            waits[4:7] if h == 0 else [lambda: None] * 3,
            [ref.at[pl.ds(h * tokens, tokens)] for ref in (q, k, v)],
        )
    waits[7]()
    share = slots * piece
    group = 2 if spread % 2 == 0 else 1
    steps = spread // group

    def blocks(h, s, count):
        return pl.ds(h * peers + s * slots, count * slots)

    def third(h, mask):
        s = moved(me_s, steps_s, mask)
        return pltpu.make_async_remote_copy(
            src_ref=rcv.at[blocks(h, s, 1)],
            dst_ref=out.at[me_s, :, h],
            send_sem=s3.at[h, mask],
            recv_sem=r3.at[h, mask],
            device_id={"space": s},
        )

    for step in range(steps - 1, -1, -1):
        size = group * share
        base = moved(me_s // group, bit_steps(me_s // group, steps), step) * group
        parts = [
            pl.ds(pl.multiple_of(h * tokens + base * share, size), size) for h in range(halves)
        ]

        def attend_pair(index, carry):
            cols = pl.ds(pl.multiple_of(index * LANES, LANES), LANES)
            queries = jnp.concatenate([q[part, cols] for part in parts], 0)
            result = attend(queries, k[:, cols], v[:, cols], None)
            for h, part in enumerate(parts):
                a[part, cols] = result[h * size : (h + 1) * size]
            return carry

        lax.fori_loop(0, width // LANES, attend_pair, 0, unroll=UNROLL_S)
        added = project(jnp.concatenate([a[part] for part in parts], 0), weights[7][...])
        for h in range(halves):
            here = blocks(h, base, group)
            new = added[h * size : (h + 1) * size].reshape(group * slots, piece, width)
            rcv[here] = (rcv[here].astype(F32) + new).astype(BF16)
        for member in range(group - 1, -1, -1):
            if step * group + member:
                for h in range(halves):
                    third(h, step * group + member).start()
    last = [
        pltpu.make_async_copy(rcv.at[blocks(h, me_s, 1)], out.at[me_s, :, h], lsem.at[h])
        for h in range(halves)
    ]
    for copy in last:
        copy.start()
    for h in range(halves):
        for mask in range(1, slots):
            first(h, mask).wait_send()

    for h in range(halves):
        for mask in everyone:
            for core in range(2):
                second_wait(h, mask, core).wait_send()
        second_wait(h, 0, 0).wait_send()
    for h in range(halves):
        for mask in range(1, spread):
            third(h, mask).wait()
        last[h].wait()


def run_layer(frames_in, slots, spread, norms, weights):
    rows, patches, width = frames_in.shape
    frames, places, halves = rows * slots, patches // slots, 2
    piece = places // halves
    total = frames * places
    vmem, hbm = pl.BlockSpec(memory_space=pltpu.VMEM), pl.BlockSpec(memory_space=pltpu.HBM)
    dma = pltpu.SemaphoreType.DMA
    return pl.pallas_call(
        functools.partial(layer_kernel, slots, spread),
        out_shape=jax.ShapeDtypeStruct((rows, slots, halves, piece, width), BF16),
        in_specs=[hbm] + [vmem] * 4 + [hbm] * 8,
        out_specs=hbm,
        scratch_shapes=[
            pltpu.VMEM((8, width, width), BF16),
            pltpu.VMEM((halves, frames, piece, width), BF16),
            pltpu.VMEM((halves, frames, piece, width), BF16),
            pltpu.VMEM((total // piece, piece, width), BF16),
        ]
        + [pltpu.VMEM((total, width), BF16)] * 4
        + [
            dma((8,)),
            dma((halves,)),
            dma((halves, slots)),
            dma((halves, slots)),
            dma((halves, slots * spread // 2, 2)),
            dma((halves, slots * spread // 2, 2)),
            dma((halves, spread)),
            dma((halves, spread)),
        ],
        compiler_params=pltpu.CompilerParams(
            collective_id=0, has_side_effects=True, vmem_limit_bytes=60 << 20
        ),
    )(
        frames_in.reshape(rows, slots, halves, piece, width),
        *[norm.reshape(1, -1) for norm in norms],
        *weights,
    ).reshape(frames_in.shape)


def split_heads(tokens):
    return tokens.reshape(tokens.shape[0], tokens.shape[1], tokens.shape[2] // HEAD_DIM, HEAD_DIM)


def gathered_space(after_time, gain, shift, wq, wk, wv, wo):
    normed = layer_norm(after_time, gain, shift)
    queries = project(normed, wq).astype(BF16)
    everywhere = lax.all_gather(normed, "space", axis=1, tiled=True)
    keys_in, values_in = (project(everywhere, w).astype(BF16) for w in (wk, wv))
    scores = 0.125 * jnp.einsum(
        "fqhd,fkhd->fhqk", split_heads(queries), split_heads(keys_in), preferred_element_type=F32
    )
    weights = jax.nn.softmax(scores, axis=-1).astype(BF16)
    spatial = jnp.einsum(
        "fhqk,fkhd->fqhd", weights, split_heads(values_in), preferred_element_type=F32
    )
    spatial = spatial.astype(BF16).reshape(after_time.shape)
    return (after_time.astype(F32) + project(spatial, wo)).astype(BF16)


def body(frames_in, tg, ts, tq, tk, tv, to, sg, ss, sq, sk, sv, so):
    slots, spread = lax.axis_size("tm"), lax.axis_size("space")
    rows, patches, width = frames_in.shape
    frames, places = rows * slots, patches // slots
    if rows == spread and spread % 2 == 0 and not (slots & (slots - 1) or spread & (spread - 1)):
        return run_layer(
            frames_in, slots, spread, (tg, ts, sg, ss), (tq, tk, tv, to, sq, sk, sv, so)
        )
    tokens = lax.all_to_all(
        frames_in.reshape(rows, slots, places, width), "tm", split_axis=1, concat_axis=0, tiled=True
    ).reshape(frames * places, width)
    after = run_branch(functools.partial(time_branch, frames), tokens, tg, ts, tq, tk, tv, to)
    after = lax.all_to_all(
        after.reshape(frames, 1, places, width), "tm", split_axis=0, concat_axis=1, tiled=True
    ).reshape(rows, patches, width)
    return gathered_space(after, sg, ss, sq, sk, sv, so)


def solution(mesh):
    return jax.shard_map(
        body,
        mesh=mesh,
        in_specs=(P("tm", "space", None),) + (P(),) * 12,
        out_specs=P("tm", "space", None),
        check_vma=False,
    )
```

```python
import functools
import math

import jax
import jax.numpy as jnp
from jax import lax
from jax.experimental import pallas as pl
from jax.experimental.pallas import tpu as pltpu
from jax.sharding import PartitionSpec as P

HEAD_DIM = 64
LANES = 128
UNROLL_T, UNROLL_S = 8, 8
SCALE = 0.125 * math.log2(math.e)
F32, BF16 = jnp.float32, jnp.bfloat16


def layer_norm(tokens, gain, shift):
    values = tokens.astype(F32)
    mean_value = jnp.mean(values, axis=-1, keepdims=True)
    centred = values - mean_value
    variance = jnp.mean(centred * centred, axis=-1, keepdims=True)
    return (centred * lax.rsqrt(variance + 1e-05) * gain + shift).astype(BF16)


def project(tokens, weight):
    return jnp.dot(tokens, weight, preferred_element_type=F32)


def permutation(rows, inner, outer, back):
    row = lax.broadcasted_iota(jnp.int32, (rows, rows), 1 if back else 0)
    col = lax.broadcasted_iota(jnp.int32, (rows, rows), 0 if back else 1)
    return jnp.where((row % inner) * outer + row // inner == col, 1.0, 0.0).astype(BF16)


def lane_masks(width):
    lane = lax.broadcasted_iota(jnp.int32, (1, LANES), 1)
    return [(lane // HEAD_DIM == part) for part in range(LANES // HEAD_DIM)]


def attend(queries, keys_in, values_in, same):
    rows = queries.shape[0]
    masks = lane_masks(LANES)
    own = jnp.concatenate([jnp.where(mask, queries, jnp.zeros_like(queries)) for mask in masks], 0)
    scores = lax.dot_general(own, keys_in, (((1,), (1,)), ((), ())), preferred_element_type=F32)
    if same is not None:
        scores = jnp.where(jnp.concatenate([same] * len(masks), 0), scores, -1e30)
    top = jnp.max(scores, axis=-1, keepdims=True)
    weights = jnp.exp2((scores - top) * SCALE).astype(BF16)
    both = jnp.concatenate([values_in, jnp.ones_like(values_in)], 1)
    added = jnp.dot(weights, both, preferred_element_type=F32)
    added = added[:, :LANES] / added[:, LANES:]
    result = added[:rows]
    for part in range(1, len(masks)):
        result = jnp.where(masks[part], added[part * rows : (part + 1) * rows], result)
    return result.astype(BF16)


def qkv(normed, weights, waits, outs):
    for weight, wait, out in zip(weights, waits, outs):
        wait()
        out[...] = project(normed, weight[...]).astype(BF16)


def time_branch(frames, x, gain, shift, weights, waits, q, k, v, a):
    rows, width = q.shape
    places = rows // frames
    order = permutation(rows, frames, places, False)
    x = project(order, x).astype(BF16)
    qkv(layer_norm(x, gain, shift), weights[:3], waits[:3], (q, k, v))
    size = max(frames, LANES)
    same = (
        lax.broadcasted_iota(jnp.int32, (size, size), 0) // frames
        == lax.broadcasted_iota(jnp.int32, (size, size), 1) // frames
    )

    def pair(index, carry):
        cols = pl.ds(pl.multiple_of(index * LANES, LANES), LANES)
        for group in range(rows // size):
            part = (pl.ds(group * size, size), cols)
            a[part] = attend(q[part], k[part], v[part], same)
        return carry

    lax.fori_loop(0, width // LANES, pair, 0, unroll=UNROLL_T)
    waits[3]()
    after = (x.astype(F32) + project(a[...], weights[3][...])).astype(BF16)
    return project(permutation(rows, frames, places, True), after)


def branch_kernel(branch, x, gain, shift, w0, w1, w2, w3, out, held, q, k, v, a, sems):
    copies = [
        pltpu.make_async_copy(w, held.at[i], sems.at[i]) for i, w in enumerate((w0, w1, w2, w3))
    ]
    for copy in copies:
        copy.start()
    weights = [held.at[i] for i in range(4)]
    waits = [copy.wait for copy in copies]
    out[...] = branch(x[...], gain[...], shift[...], weights, waits, q, k, v, a).astype(BF16)


def run_branch(branch, x, gain, shift, *weights):
    rows, width = x.shape
    vmem = pl.BlockSpec(memory_space=pltpu.VMEM)
    return pl.pallas_call(
        functools.partial(branch_kernel, branch),
        out_shape=jax.ShapeDtypeStruct((rows, width), BF16),
        in_specs=[vmem] * 3 + [pl.BlockSpec(memory_space=pl.ANY)] * 4,
        out_specs=vmem,
        scratch_shapes=[pltpu.VMEM((4, width, width), BF16)]
        + [pltpu.VMEM((rows, width), BF16)] * 4
        + [pltpu.SemaphoreType.DMA((4,))],
        compiler_params=pltpu.CompilerParams(vmem_limit_bytes=60 << 20),
    )(x, gain.reshape(1, -1), shift.reshape(1, -1), *weights)


def bit_steps(index, count):
    out, bit = [], 1
    while bit < count:
        out.append((bit, bit - 2 * bit * ((index // bit) % 2)))
        bit *= 2
    return out


def moved(index, steps, mask):
    for bit, step in steps:
        if mask & bit:
            index = index + step
    return index


def one_hot(shape, source):
    row = lax.broadcasted_iota(jnp.int32, shape, 0)
    col = lax.broadcasted_iota(jnp.int32, shape, 1)
    return jnp.where(source(row) == col, 1.0, 0.0).astype(BF16)


def flat(block):
    return block.astype(F32).reshape(-1, block.shape[-1]).astype(BF16)


def layer_kernel(
    slots,
    spread,
    x,
    tg,
    ts,
    sg,
    ss,
    *refs,
):
    sources, out = refs[:8], refs[8]
    held, xv, xs, xt, snd, rcv, res, q, k, v, a, wsem, lsem, s1, r1, s2, r2, s3, r3 = refs[9:]
    me_t, me_s = lax.axis_index("tm"), lax.axis_index("space")
    halves, rows, _, piece, width = xv.shape
    chunks, size, _ = xt.shape
    frames = rows * slots
    few = size // frames
    fold = piece // few
    peers = slots * spread
    chips = spread // 2
    tokens = frames * piece
    me_c = me_s % 2
    me_z = me_s // 2
    steps_t, steps_s = bit_steps(me_t, slots), bit_steps(me_s, spread)
    steps_z = bit_steps(me_z, chips)

    halves_in = [pltpu.make_async_copy(x.at[:, :, h], xv.at[h], lsem.at[h]) for h in range(halves)]
    loads = [pltpu.make_async_copy(w, held.at[i], wsem.at[i]) for i, w in enumerate(sources)]
    halves_in[0].start()
    barrier = pltpu.get_barrier_semaphore()
    for mask in range(1, peers):
        pl.semaphore_signal(
            barrier,
            inc=1,
            device_id={
                "tm": moved(me_t, steps_t, mask % slots),
                "space": moved(me_s, steps_s, mask // slots),
            },
        )
    for copy in halves_in[1:] + loads:
        copy.start()

    def first(c, mask):
        t = moved(me_t, steps_t, mask)
        return pltpu.make_async_remote_copy(
            src_ref=xs.at[c, t],
            dst_ref=xt.at[c, pl.ds(me_t * rows * few, rows * few)],
            send_sem=s1.at[c],
            recv_sem=r1.at[c],
            device_id={"tm": t},
        )

    def first_all(c):
        part = xt.at[c, pl.ds(0, (slots - 1) * rows * few)]
        return pltpu.make_async_remote_copy(
            src_ref=part,
            dst_ref=part,
            send_sem=s1.at[c],
            recv_sem=r1.at[c],
            device_id={"tm": moved(me_t, steps_t, 1)},
        )

    def second(c, mask, core):
        t, z = moved(me_t, steps_t, mask % slots), moved(me_z, steps_z, mask // slots)
        return pltpu.make_async_remote_copy(
            src_ref=snd.at[c, (t * chips + z) * 2 + core],
            dst_ref=rcv.at[c, me_s * slots + me_t],
            send_sem=s2.at[c],
            recv_sem=r2.at[c],
            device_id={"tm": t, "space": z * 2 + core},
        )

    def second_all(c):
        part = rcv.at[c, pl.ds(0, peers - 1)]
        return pltpu.make_async_remote_copy(
            src_ref=part,
            dst_ref=part,
            send_sem=s2.at[c],
            recv_sem=r2.at[c],
            device_id={"space": me_s + 1 - 2 * me_c},
        )

    def home_row(r):
        block = rows * few
        chunk, slot, frame, place = r // (slots * block), (r // block) % slots, (r // few) % rows, r % few
        return (frame * slots + slot) * piece + chunk * few + place

    per_half = rows * slots * piece
    for h in range(halves):
        halves_in[h].wait()
        moved_in = project(one_hot((per_half, per_half), home_row), flat(xv[h])).astype(BF16)
        for n in range(fold):
            c = h * fold + n
            for t in range(slots):
                start = (n * slots + t) * rows * few
                xs[c, t] = moved_in[start : start + rows * few]
            xt[c, pl.ds(me_t * rows * few, rows * few)] = xs[c, me_t]
        if h == 0:
            pl.semaphore_wait(barrier, peers - 1)
        for n in range(fold):
            for mask in range(slots - 1, 0, -1):
                first(h * fold + n, mask).start()

    weights = [held.at[i] for i in range(8)]
    waits = [copy.wait for copy in loads]
    same = (
        lax.broadcasted_iota(jnp.int32, (size, size), 0) % few
        == lax.broadcasted_iota(jnp.int32, (size, size), 1) % few
    )
    folding = one_hot(
        (fold * size, fold * size),
        lambda r: ((r // few) % fold) * size + (r // piece) * few + r % few,
    )
    columns = width // fold

    def send(c, core):
        for mask in range(slots * chips - 1, 0, -1):
            second(c, mask, core).start()

    for c in range(chunks):
        first_all(c).wait_recv()
        part = pl.ds(0, size)
        tok = xt[c]
        qkv(
            layer_norm(tok, tg[...], ts[...]),
            weights[:3],
            waits[:3] if c == 0 else [lambda: None] * 3,
            [ref.at[part] for ref in (q, k, v)],
        )

        def time_pair(index, carry):
            cols = pl.ds(pl.multiple_of(index * LANES, LANES), LANES)
            a[part, cols] = attend(q[part, cols], k[part, cols], v[part, cols], same)
            return carry

        lax.fori_loop(0, width // LANES, time_pair, 0, unroll=UNROLL_T)
        if c == 0:
            waits[3]()
        after = (tok.astype(F32) + project(a[part], weights[3][...])).astype(BF16)
        after = jnp.concatenate([after[:, n * columns : (n + 1) * columns] for n in range(fold)], 0)
        snd[c] = project(folding, after).reshape(frames, piece, columns).astype(BF16)
        send(c, 0)
        pltpu.make_async_remote_copy(
            src_ref=snd.at[c, (me_t * chips + me_z) * 2 + 1 - me_c],
            dst_ref=rcv.at[c, me_s * slots + me_t],
            send_sem=s2.at[c],
            recv_sem=r2.at[c],
            device_id={"space": me_z * 2 + 1 - me_c},
        ).start()
        rcv[c, me_s * slots + me_t] = snd[c, me_t * rows + me_s]
    for c in range(chunks):
        send(c, 1)

    for h in range(halves):
        for n in range(fold):
            second_all(h * fold + n).wait_recv()
        arrived = jnp.concatenate([flat(rcv[h * fold + n]) for n in range(fold)], 0)
        frame = jnp.concatenate(
            [
                project(
                    one_hot(
                        (tokens, fold * tokens),
                        lambda r: ((r // few) % fold) * tokens + (r // piece) * piece + n * few + r % few,
                    ),
                    arrived,
                ).astype(BF16)
                for n in range(fold)
            ],
            1,
        )
        res[pl.ds(h * peers, peers)] = frame.astype(F32).reshape(peers, piece, width).astype(BF16)
        qkv(
            layer_norm(frame, sg[...], ss[...]),
            weights[4:7],
            waits[4:7] if h == 0 else [lambda: None] * 3,
            [ref.at[pl.ds(h * tokens, tokens)] for ref in (q, k, v)],
        )
    waits[7]()
    share = slots * piece
    group = 2 if spread % 2 == 0 else 1
    steps = spread // group

    def blocks(h, s, count):
        return pl.ds(h * peers + s * slots, count * slots)

    def third(h, mask):
        s = moved(me_s, steps_s, mask)
        return pltpu.make_async_remote_copy(
            src_ref=res.at[blocks(h, s, 1)],
            dst_ref=out.at[me_s, :, h],
            send_sem=s3.at[h, mask],
            recv_sem=r3.at[h, mask],
            device_id={"space": s},
        )

    for step in range(steps - 1, -1, -1):
        size = group * share
        base = moved(me_s // group, bit_steps(me_s // group, steps), step) * group
        parts = [
            pl.ds(pl.multiple_of(h * tokens + base * share, size), size) for h in range(halves)
        ]

        def attend_pair(index, carry):
            cols = pl.ds(pl.multiple_of(index * LANES, LANES), LANES)
            queries = jnp.concatenate([q[part, cols] for part in parts], 0)
            result = attend(queries, k[:, cols], v[:, cols], None)
            for h, part in enumerate(parts):
                a[part, cols] = result[h * size : (h + 1) * size]
            return carry

        lax.fori_loop(0, width // LANES, attend_pair, 0, unroll=UNROLL_S)
        added = project(jnp.concatenate([a[part] for part in parts], 0), weights[7][...])
        for h in range(halves):
            here = blocks(h, base, group)
            new = added[h * size : (h + 1) * size].reshape(group * slots, piece, width)
            res[here] = (res[here].astype(F32) + new).astype(BF16)
        for member in range(group - 1, -1, -1):
            if step * group + member:
                for h in range(halves):
                    third(h, step * group + member).start()
    last = [
        pltpu.make_async_copy(res.at[blocks(h, me_s, 1)], out.at[me_s, :, h], lsem.at[h])
        for h in range(halves)
    ]
    for copy in last:
        copy.start()
    for c in range(chunks):
        first_all(c).wait_send()
        second_all(c).wait_send()
    for h in range(halves):
        for mask in range(1, spread):
            third(h, mask).wait()
        last[h].wait()


def run_layer(frames_in, slots, spread, norms, weights):
    rows, patches, width = frames_in.shape
    frames, places, halves = rows * slots, patches // slots, 2
    piece = places // halves
    total = frames * places
    few = LANES // frames
    fold, size = piece // few, frames * few
    chunks = halves * fold
    vmem, hbm = pl.BlockSpec(memory_space=pltpu.VMEM), pl.BlockSpec(memory_space=pltpu.HBM)
    dma = pltpu.SemaphoreType.DMA
    return pl.pallas_call(
        functools.partial(layer_kernel, slots, spread),
        out_shape=pltpu.VMEM((rows, slots, halves, piece, width), BF16),
        in_specs=[hbm] + [vmem] * 4 + [hbm] * 8,
        out_specs=vmem,
        scratch_shapes=[
            pltpu.VMEM((8, width, width), BF16),
            pltpu.VMEM((halves, rows, slots, piece, width), BF16),
            pltpu.VMEM((chunks, slots, rows * few, width), BF16),
            pltpu.VMEM((chunks, size, width), BF16),
            pltpu.VMEM((chunks, frames, piece, width // fold), BF16),
            pltpu.VMEM((chunks, slots * spread, piece, width // fold), BF16),
            pltpu.VMEM((total // piece, piece, width), BF16),
        ]
        + [pltpu.VMEM((total, width), BF16)] * 4
        + [
            dma((8,)),
            dma((halves,)),
            dma((chunks,)),
            dma((chunks,)),
            dma((chunks,)),
            dma((chunks,)),
            dma((halves, spread)),
            dma((halves, spread)),
        ],
        compiler_params=pltpu.CompilerParams(
            collective_id=0, has_side_effects=True, vmem_limit_bytes=60 << 20
        ),
    )(
        frames_in.reshape(rows, slots, halves, piece, width),
        *[norm.reshape(1, -1) for norm in norms],
        *weights,
    ).reshape(frames_in.shape)


def split_heads(tokens):
    return tokens.reshape(tokens.shape[0], tokens.shape[1], tokens.shape[2] // HEAD_DIM, HEAD_DIM)


def gathered_space(after_time, gain, shift, wq, wk, wv, wo):
    normed = layer_norm(after_time, gain, shift)
    queries = project(normed, wq).astype(BF16)
    everywhere = lax.all_gather(normed, "space", axis=1, tiled=True)
    keys_in, values_in = (project(everywhere, w).astype(BF16) for w in (wk, wv))
    scores = 0.125 * jnp.einsum(
        "fqhd,fkhd->fhqk", split_heads(queries), split_heads(keys_in), preferred_element_type=F32
    )
    weights = jax.nn.softmax(scores, axis=-1).astype(BF16)
    spatial = jnp.einsum(
        "fhqk,fkhd->fqhd", weights, split_heads(values_in), preferred_element_type=F32
    )
    spatial = spatial.astype(BF16).reshape(after_time.shape)
    return (after_time.astype(F32) + project(spatial, wo)).astype(BF16)


def body(frames_in, tg, ts, tq, tk, tv, to, sg, ss, sq, sk, sv, so):
    slots, spread = lax.axis_size("tm"), lax.axis_size("space")
    rows, patches, width = frames_in.shape
    frames, places = rows * slots, patches // slots
    powers = not (slots & (slots - 1) or spread & (spread - 1)) and spread % 2 == 0
    tiles = places == 16 and LANES % frames == 0 and LANES // frames in (2, 4, 8)
    if rows == spread and powers and tiles:
        return run_layer(
            frames_in, slots, spread, (tg, ts, sg, ss), (tq, tk, tv, to, sq, sk, sv, so)
        )
    tokens = lax.all_to_all(
        frames_in.reshape(rows, slots, places, width), "tm", split_axis=1, concat_axis=0, tiled=True
    ).reshape(frames * places, width)
    after = run_branch(functools.partial(time_branch, frames), tokens, tg, ts, tq, tk, tv, to)
    after = lax.all_to_all(
        after.reshape(frames, 1, places, width), "tm", split_axis=0, concat_axis=1, tiled=True
    ).reshape(rows, patches, width)
    return gathered_space(after, sg, ss, sq, sk, sv, so)


def solution(mesh):
    return jax.shard_map(
        body,
        mesh=mesh,
        in_specs=(P("tm", "space", None),) + (P(),) * 12,
        out_specs=P("tm", "space", None),
        check_vma=False,
    )
```

```python
import functools
import math

import jax
import jax.numpy as jnp
from jax import lax
from jax.experimental import pallas as pl
from jax.experimental.pallas import tpu as pltpu
from jax.sharding import PartitionSpec as P

HEAD_DIM = 64
LANES = 128
UNROLL_T, UNROLL_S = 8, 8
SCALE = 0.125 * math.log2(math.e)
F32, BF16 = jnp.float32, jnp.bfloat16


def layer_norm(tokens, gain, shift):
    values = tokens.astype(F32)
    mean_value = jnp.mean(values, axis=-1, keepdims=True)
    centred = values - mean_value
    variance = jnp.mean(centred * centred, axis=-1, keepdims=True)
    return (centred * lax.rsqrt(variance + 1e-05) * gain + shift).astype(BF16)


def project(tokens, weight):
    return jnp.dot(tokens, weight, preferred_element_type=F32)


def permutation(rows, inner, outer, back):
    row = lax.broadcasted_iota(jnp.int32, (rows, rows), 1 if back else 0)
    col = lax.broadcasted_iota(jnp.int32, (rows, rows), 0 if back else 1)
    return jnp.where((row % inner) * outer + row // inner == col, 1.0, 0.0).astype(BF16)


def lane_masks(width):
    lane = lax.broadcasted_iota(jnp.int32, (1, LANES), 1)
    return [(lane // HEAD_DIM == part) for part in range(LANES // HEAD_DIM)]


def attend(queries, keys_in, values_in, same):
    rows = queries.shape[0]
    masks = lane_masks(LANES)
    own = jnp.concatenate([jnp.where(mask, queries, jnp.zeros_like(queries)) for mask in masks], 0)
    scores = lax.dot_general(own, keys_in, (((1,), (1,)), ((), ())), preferred_element_type=F32)
    if same is not None:
        scores = jnp.where(jnp.concatenate([same] * len(masks), 0), scores, -1e30)
    top = jnp.max(scores, axis=-1, keepdims=True)
    weights = jnp.exp2((scores - top) * SCALE).astype(BF16)
    both = jnp.concatenate([values_in, jnp.ones_like(values_in)], 1)
    added = jnp.dot(weights, both, preferred_element_type=F32)
    added = added[:, :LANES] / added[:, LANES:]
    result = added[:rows]
    for part in range(1, len(masks)):
        result = jnp.where(masks[part], added[part * rows : (part + 1) * rows], result)
    return result.astype(BF16)


def qkv(normed, weights, waits, outs):
    for weight, wait, out in zip(weights, waits, outs):
        wait()
        out[...] = project(normed, weight[...]).astype(BF16)


def time_branch(frames, x, gain, shift, weights, waits, q, k, v, a):
    rows, width = q.shape
    places = rows // frames
    order = permutation(rows, frames, places, False)
    x = project(order, x).astype(BF16)
    qkv(layer_norm(x, gain, shift), weights[:3], waits[:3], (q, k, v))
    size = max(frames, LANES)
    same = (
        lax.broadcasted_iota(jnp.int32, (size, size), 0) // frames
        == lax.broadcasted_iota(jnp.int32, (size, size), 1) // frames
    )

    def pair(index, carry):
        cols = pl.ds(pl.multiple_of(index * LANES, LANES), LANES)
        for group in range(rows // size):
            part = (pl.ds(group * size, size), cols)
            a[part] = attend(q[part], k[part], v[part], same)
        return carry

    lax.fori_loop(0, width // LANES, pair, 0, unroll=UNROLL_T)
    waits[3]()
    after = (x.astype(F32) + project(a[...], weights[3][...])).astype(BF16)
    return project(permutation(rows, frames, places, True), after)


def branch_kernel(branch, x, gain, shift, w0, w1, w2, w3, out, held, q, k, v, a, sems):
    copies = [
        pltpu.make_async_copy(w, held.at[i], sems.at[i]) for i, w in enumerate((w0, w1, w2, w3))
    ]
    for copy in copies:
        copy.start()
    weights = [held.at[i] for i in range(4)]
    waits = [copy.wait for copy in copies]
    out[...] = branch(x[...], gain[...], shift[...], weights, waits, q, k, v, a).astype(BF16)


def run_branch(branch, x, gain, shift, *weights):
    rows, width = x.shape
    vmem = pl.BlockSpec(memory_space=pltpu.VMEM)
    return pl.pallas_call(
        functools.partial(branch_kernel, branch),
        out_shape=jax.ShapeDtypeStruct((rows, width), BF16),
        in_specs=[vmem] * 3 + [pl.BlockSpec(memory_space=pl.ANY)] * 4,
        out_specs=vmem,
        scratch_shapes=[pltpu.VMEM((4, width, width), BF16)]
        + [pltpu.VMEM((rows, width), BF16)] * 4
        + [pltpu.SemaphoreType.DMA((4,))],
        compiler_params=pltpu.CompilerParams(vmem_limit_bytes=60 << 20),
    )(x, gain.reshape(1, -1), shift.reshape(1, -1), *weights)


def bit_steps(index, count):
    out, bit = [], 1
    while bit < count:
        out.append((bit, bit - 2 * bit * ((index // bit) % 2)))
        bit *= 2
    return out


def moved(index, steps, mask):
    for bit, step in steps:
        if mask & bit:
            index = index + step
    return index


def one_hot(shape, source):
    row = lax.broadcasted_iota(jnp.int32, shape, 0)
    col = lax.broadcasted_iota(jnp.int32, shape, 1)
    return jnp.where(source(row) == col, 1.0, 0.0).astype(BF16)


def flat(block):
    return block.astype(F32).reshape(-1, block.shape[-1]).astype(BF16)


def layer_kernel(
    slots,
    spread,
    x,
    *refs,
):
    scales, sources, out = refs[:4], refs[4:12], refs[12]
    norms, held, xv, xs, xt, snd, rcv, res, q, k, v, a, nsem, wsem, lsem, s1, r1, s2, r2, s3, r3 = refs[13:]
    me_t, me_s = lax.axis_index("tm"), lax.axis_index("space")
    halves, rows, _, piece, width = xv.shape
    chunks, size, _ = xt.shape
    frames = rows * slots
    few = size // frames
    fold = piece // few
    peers = slots * spread
    chips = spread // 2
    tokens = frames * piece
    me_c = me_s % 2
    me_z = me_s // 2
    steps_t, steps_s = bit_steps(me_t, slots), bit_steps(me_s, spread)
    steps_z = bit_steps(me_z, chips)

    halves_in = [pltpu.make_async_copy(x.at[:, :, h], xv.at[h], lsem.at[h]) for h in range(halves)]
    loads = [pltpu.make_async_copy(w, held.at[i], wsem.at[i]) for i, w in enumerate(sources)]
    norms_in = [pltpu.make_async_copy(n, norms.at[i], nsem.at[i]) for i, n in enumerate(scales)]
    halves_in[0].start()
    barrier = pltpu.get_barrier_semaphore()
    for mask in range(1, peers):
        pl.semaphore_signal(
            barrier,
            inc=1,
            device_id={
                "tm": moved(me_t, steps_t, mask % slots),
                "space": moved(me_s, steps_s, mask // slots),
            },
        )
    for copy in halves_in[1:] + norms_in + loads:
        copy.start()

    def first(c, mask):
        t = moved(me_t, steps_t, mask)
        return pltpu.make_async_remote_copy(
            src_ref=xs.at[c, t],
            dst_ref=xt.at[c, pl.ds(me_t * rows * few, rows * few)],
            send_sem=s1.at[c],
            recv_sem=r1.at[c],
            device_id={"tm": t},
        )

    def first_all(c):
        part = xt.at[c, pl.ds(0, (slots - 1) * rows * few)]
        return pltpu.make_async_remote_copy(
            src_ref=part,
            dst_ref=part,
            send_sem=s1.at[c],
            recv_sem=r1.at[c],
            device_id={"tm": moved(me_t, steps_t, 1)},
        )

    def second(c, mask, core):
        t, z = moved(me_t, steps_t, mask % slots), moved(me_z, steps_z, mask // slots)
        return pltpu.make_async_remote_copy(
            src_ref=snd.at[c, (t * chips + z) * 2 + core],
            dst_ref=rcv.at[c, me_s * slots + me_t],
            send_sem=s2.at[c],
            recv_sem=r2.at[c],
            device_id={"tm": t, "space": z * 2 + core},
        )

    def second_all(c):
        part = rcv.at[c, pl.ds(0, peers - 1)]
        return pltpu.make_async_remote_copy(
            src_ref=part,
            dst_ref=part,
            send_sem=s2.at[c],
            recv_sem=r2.at[c],
            device_id={"space": me_s + 1 - 2 * me_c},
        )

    def home_row(r):
        block = rows * few
        chunk, slot, frame, place = r // (slots * block), (r // block) % slots, (r // few) % rows, r % few
        return (frame * slots + slot) * piece + chunk * few + place

    per_half = rows * slots * piece
    for h in range(halves):
        halves_in[h].wait()
        moved_in = project(one_hot((per_half, per_half), home_row), flat(xv[h])).astype(BF16)
        for n in range(fold):
            c = h * fold + n
            for t in range(slots):
                start = (n * slots + t) * rows * few
                xs[c, t] = moved_in[start : start + rows * few]
            xt[c, pl.ds(me_t * rows * few, rows * few)] = xs[c, me_t]
        if h == 0:
            pl.semaphore_wait(barrier, peers - 1)
        for n in range(fold):
            for mask in range(slots - 1, 0, -1):
                first(h * fold + n, mask).start()

    weights = [held.at[i] for i in range(8)]
    waits = [copy.wait for copy in loads]
    for copy in norms_in:
        copy.wait()
    tg, ts, sg, ss = [norms.at[i] for i in range(4)]
    same = (
        lax.broadcasted_iota(jnp.int32, (size, size), 0) % few
        == lax.broadcasted_iota(jnp.int32, (size, size), 1) % few
    )
    folding = one_hot(
        (fold * size, fold * size),
        lambda r: ((r // few) % fold) * size + (r // piece) * few + r % few,
    )
    columns = width // fold

    def send(c, core):
        for mask in range(slots * chips - 1, 0, -1):
            second(c, mask, core).start()

    for c in range(chunks):
        first_all(c).wait_recv()
        part = pl.ds(0, size)
        tok = xt[c]
        qkv(
            layer_norm(tok, tg[...], ts[...]),
            weights[:3],
            waits[:3] if c == 0 else [lambda: None] * 3,
            [ref.at[part] for ref in (q, k, v)],
        )

        def time_pair(index, carry):
            cols = pl.ds(pl.multiple_of(index * LANES, LANES), LANES)
            a[part, cols] = attend(q[part, cols], k[part, cols], v[part, cols], same)
            return carry

        lax.fori_loop(0, width // LANES, time_pair, 0, unroll=UNROLL_T)
        if c == 0:
            waits[3]()
        after = (tok.astype(F32) + project(a[part], weights[3][...])).astype(BF16)
        after = jnp.concatenate([after[:, n * columns : (n + 1) * columns] for n in range(fold)], 0)
        snd[c] = project(folding, after).reshape(frames, piece, columns).astype(BF16)
        send(c, 0)
        pltpu.make_async_remote_copy(
            src_ref=snd.at[c, (me_t * chips + me_z) * 2 + 1 - me_c],
            dst_ref=rcv.at[c, me_s * slots + me_t],
            send_sem=s2.at[c],
            recv_sem=r2.at[c],
            device_id={"space": me_z * 2 + 1 - me_c},
        ).start()
        rcv[c, me_s * slots + me_t] = snd[c, me_t * rows + me_s]
    for c in range(chunks):
        send(c, 1)

    for h in range(halves):
        for n in range(fold):
            second_all(h * fold + n).wait_recv()
        arrived = jnp.concatenate([flat(rcv[h * fold + n]) for n in range(fold)], 0)
        frame = jnp.concatenate(
            [
                project(
                    one_hot(
                        (tokens, fold * tokens),
                        lambda r: ((r // few) % fold) * tokens + (r // piece) * piece + n * few + r % few,
                    ),
                    arrived,
                ).astype(BF16)
                for n in range(fold)
            ],
            1,
        )
        res[:, :, h] = frame.astype(F32).reshape(spread, slots, piece, width).astype(BF16)
        qkv(
            layer_norm(frame, sg[...], ss[...]),
            weights[4:7],
            waits[4:7] if h == 0 else [lambda: None] * 3,
            [ref.at[pl.ds(h * tokens, tokens)] for ref in (q, k, v)],
        )
    waits[7]()
    share = slots * piece
    both = 2 * share

    def third(target):
        return pltpu.make_async_remote_copy(
            src_ref=res.at[target],
            dst_ref=out.at[me_s],
            send_sem=s3,
            recv_sem=r3,
            device_id={"space": target},
        )

    near = chips // 2
    targets = [(1 - me_z // near) * near + n for n in range(near)] if near else []
    targets += [moved(me_z, steps_z, mask) for mask in range(near - 1, 0, -1)]
    for target in targets + [me_z]:
        parts = [
            pl.ds(pl.multiple_of(h * tokens + target * both, both), both) for h in range(halves)
        ]

        def attend_pair(index, carry):
            cols = pl.ds(pl.multiple_of(index * LANES, LANES), LANES)
            queries = jnp.concatenate([q[part, cols] for part in parts], 0)
            result = attend(queries, k[:, cols], v[:, cols], None)
            for h, part in enumerate(parts):
                a[part, cols] = result[h * both : (h + 1) * both]
            return carry

        lax.fori_loop(0, width // LANES, attend_pair, 0, unroll=UNROLL_S)
        added = project(jnp.concatenate([a[part] for part in parts], 0), weights[7][...])
        here = pl.ds(2 * target, 2)
        for h in range(halves):
            new = added[h * both : (h + 1) * both].reshape(2, slots, piece, width)
            res[here, :, h] = (res[here, :, h].astype(F32) + new).astype(BF16)
        if target is me_z:
            third(me_s + 1 - 2 * me_c).start()
        else:
            for core in range(2):
                third(2 * target + core).start()
    last = pltpu.make_async_copy(res.at[me_s], out.at[me_s], lsem.at[0])
    last.start()
    for c in range(chunks):
        first_all(c).wait_send()
        second_all(c).wait_send()
    others = pl.ds(0, spread - 1)
    pltpu.make_async_remote_copy(
        src_ref=res.at[others],
        dst_ref=out.at[others],
        send_sem=s3,
        recv_sem=r3,
        device_id={"space": me_s + 1 - 2 * me_c},
    ).wait()
    last.wait()


def run_layer(frames_in, slots, spread, norms, weights):
    rows, patches, width = frames_in.shape
    frames, places, halves = rows * slots, patches // slots, 2
    piece = places // halves
    total = frames * places
    few = LANES // frames
    fold, size = piece // few, frames * few
    chunks = halves * fold
    vmem, hbm = pl.BlockSpec(memory_space=pltpu.VMEM), pl.BlockSpec(memory_space=pltpu.HBM)
    dma = pltpu.SemaphoreType.DMA
    return pl.pallas_call(
        functools.partial(layer_kernel, slots, spread),
        out_shape=pltpu.VMEM((rows, slots, halves, piece, width), BF16),
        in_specs=[hbm] * 13,
        out_specs=vmem,
        scratch_shapes=[
            pltpu.VMEM((4, 1, width), F32),
            pltpu.VMEM((8, width, width), BF16),
            pltpu.VMEM((halves, rows, slots, piece, width), BF16),
            pltpu.VMEM((chunks, slots, rows * few, width), BF16),
            pltpu.VMEM((chunks, size, width), BF16),
            pltpu.VMEM((chunks, frames, piece, width // fold), BF16),
            pltpu.VMEM((chunks, slots * spread, piece, width // fold), BF16),
            pltpu.VMEM((spread, slots, halves, piece, width), BF16),
        ]
        + [pltpu.VMEM((total, width), BF16)] * 4
        + [
            dma((4,)),
            dma((8,)),
            dma((halves,)),
            dma((chunks,)),
            dma((chunks,)),
            dma((chunks,)),
            dma((chunks,)),
            dma(()),
            dma(()),
        ],
        compiler_params=pltpu.CompilerParams(
            collective_id=0, has_side_effects=True, vmem_limit_bytes=60 << 20
        ),
    )(
        frames_in.reshape(rows, slots, halves, piece, width),
        *[norm.reshape(1, -1) for norm in norms],
        *weights,
    ).reshape(frames_in.shape)


def split_heads(tokens):
    return tokens.reshape(tokens.shape[0], tokens.shape[1], tokens.shape[2] // HEAD_DIM, HEAD_DIM)


def gathered_space(after_time, gain, shift, wq, wk, wv, wo):
    normed = layer_norm(after_time, gain, shift)
    queries = project(normed, wq).astype(BF16)
    everywhere = lax.all_gather(normed, "space", axis=1, tiled=True)
    keys_in, values_in = (project(everywhere, w).astype(BF16) for w in (wk, wv))
    scores = 0.125 * jnp.einsum(
        "fqhd,fkhd->fhqk", split_heads(queries), split_heads(keys_in), preferred_element_type=F32
    )
    weights = jax.nn.softmax(scores, axis=-1).astype(BF16)
    spatial = jnp.einsum(
        "fhqk,fkhd->fqhd", weights, split_heads(values_in), preferred_element_type=F32
    )
    spatial = spatial.astype(BF16).reshape(after_time.shape)
    return (after_time.astype(F32) + project(spatial, wo)).astype(BF16)


def body(frames_in, tg, ts, tq, tk, tv, to, sg, ss, sq, sk, sv, so):
    slots, spread = lax.axis_size("tm"), lax.axis_size("space")
    rows, patches, width = frames_in.shape
    frames, places = rows * slots, patches // slots
    powers = not (slots & (slots - 1) or spread & (spread - 1)) and spread % 2 == 0
    tiles = places == 16 and LANES % frames == 0 and LANES // frames in (2, 4, 8)
    if rows == spread and powers and tiles:
        return run_layer(
            frames_in, slots, spread, (tg, ts, sg, ss), (tq, tk, tv, to, sq, sk, sv, so)
        )
    tokens = lax.all_to_all(
        frames_in.reshape(rows, slots, places, width), "tm", split_axis=1, concat_axis=0, tiled=True
    ).reshape(frames * places, width)
    after = run_branch(functools.partial(time_branch, frames), tokens, tg, ts, tq, tk, tv, to)
    after = lax.all_to_all(
        after.reshape(frames, 1, places, width), "tm", split_axis=0, concat_axis=1, tiled=True
    ).reshape(rows, patches, width)
    return gathered_space(after, sg, ss, sq, sk, sv, so)


def solution(mesh):
    return jax.shard_map(
        body,
        mesh=mesh,
        in_specs=(P("tm", "space", None),) + (P(),) * 12,
        out_specs=P("tm", "space", None),
        check_vma=False,
    )
```

```python
import functools
import math

import jax
import jax.numpy as jnp
from jax import lax
from jax.experimental import pallas as pl
from jax.experimental.pallas import tpu as pltpu
from jax.sharding import PartitionSpec as P

HEAD_DIM = 64
LANES = 128
UNROLL_T, UNROLL_S = 8, 8
PLAN = ((4, 4), (4, 4))
EARLY = (3, 3, 0, 0)
SCALE = 0.125 * math.log2(math.e)
F32, BF16 = jnp.float32, jnp.bfloat16


def layer_norm(tokens, gain, shift):
    values = tokens.astype(F32)
    mean_value = jnp.mean(values, axis=-1, keepdims=True)
    centred = values - mean_value
    variance = jnp.mean(centred * centred, axis=-1, keepdims=True)
    return (centred * lax.rsqrt(variance + 1e-05) * gain + shift).astype(BF16)


def project(tokens, weight):
    return jnp.dot(tokens, weight, preferred_element_type=F32)


def permutation(rows, inner, outer, back):
    row = lax.broadcasted_iota(jnp.int32, (rows, rows), 1 if back else 0)
    col = lax.broadcasted_iota(jnp.int32, (rows, rows), 0 if back else 1)
    return jnp.where((row % inner) * outer + row // inner == col, 1.0, 0.0).astype(BF16)


def lane_masks(width):
    lane = lax.broadcasted_iota(jnp.int32, (1, LANES), 1)
    return [(lane // HEAD_DIM == part) for part in range(LANES // HEAD_DIM)]


def attend(queries, keys_in, values_in, same):
    rows = queries.shape[0]
    masks = lane_masks(LANES)
    own = jnp.concatenate([jnp.where(mask, queries, jnp.zeros_like(queries)) for mask in masks], 0)
    scores = lax.dot_general(own, keys_in, (((1,), (1,)), ((), ())), preferred_element_type=F32)
    if same is not None:
        scores = jnp.where(jnp.concatenate([same] * len(masks), 0), scores, -1e30)
    top = jnp.max(scores, axis=-1, keepdims=True)
    weights = jnp.exp2((scores - top) * SCALE).astype(BF16)
    both = jnp.concatenate([values_in, jnp.ones_like(values_in)], 1)
    added = jnp.dot(weights, both, preferred_element_type=F32)
    added = added[:, :LANES] / added[:, LANES:]
    result = added[:rows]
    for part in range(1, len(masks)):
        result = jnp.where(masks[part], added[part * rows : (part + 1) * rows], result)
    return result.astype(BF16)


def qkv(normed, weights, waits, outs):
    for weight, wait, out in zip(weights, waits, outs):
        wait()
        out[...] = project(normed, weight[...]).astype(BF16)


def time_branch(frames, x, gain, shift, weights, waits, q, k, v, a):
    rows, width = q.shape
    places = rows // frames
    order = permutation(rows, frames, places, False)
    x = project(order, x).astype(BF16)
    qkv(layer_norm(x, gain, shift), weights[:3], waits[:3], (q, k, v))
    size = max(frames, LANES)
    same = (
        lax.broadcasted_iota(jnp.int32, (size, size), 0) // frames
        == lax.broadcasted_iota(jnp.int32, (size, size), 1) // frames
    )

    def pair(index, carry):
        cols = pl.ds(pl.multiple_of(index * LANES, LANES), LANES)
        for group in range(rows // size):
            part = (pl.ds(group * size, size), cols)
            a[part] = attend(q[part], k[part], v[part], same)
        return carry

    lax.fori_loop(0, width // LANES, pair, 0, unroll=UNROLL_T)
    waits[3]()
    after = (x.astype(F32) + project(a[...], weights[3][...])).astype(BF16)
    return project(permutation(rows, frames, places, True), after)


def branch_kernel(branch, x, gain, shift, w0, w1, w2, w3, out, held, q, k, v, a, sems):
    copies = [
        pltpu.make_async_copy(w, held.at[i], sems.at[i]) for i, w in enumerate((w0, w1, w2, w3))
    ]
    for copy in copies:
        copy.start()
    weights = [held.at[i] for i in range(4)]
    waits = [copy.wait for copy in copies]
    out[...] = branch(x[...], gain[...], shift[...], weights, waits, q, k, v, a).astype(BF16)


def run_branch(branch, x, gain, shift, *weights):
    rows, width = x.shape
    vmem = pl.BlockSpec(memory_space=pltpu.VMEM)
    return pl.pallas_call(
        functools.partial(branch_kernel, branch),
        out_shape=jax.ShapeDtypeStruct((rows, width), BF16),
        in_specs=[vmem] * 3 + [pl.BlockSpec(memory_space=pl.ANY)] * 4,
        out_specs=vmem,
        scratch_shapes=[pltpu.VMEM((4, width, width), BF16)]
        + [pltpu.VMEM((rows, width), BF16)] * 4
        + [pltpu.SemaphoreType.DMA((4,))],
        compiler_params=pltpu.CompilerParams(vmem_limit_bytes=60 << 20),
    )(x, gain.reshape(1, -1), shift.reshape(1, -1), *weights)


def bit_steps(index, count):
    out, bit = [], 1
    while bit < count:
        out.append((bit, bit - 2 * bit * ((index // bit) % 2)))
        bit *= 2
    return out


def moved(index, steps, mask):
    for bit, step in steps:
        if mask & bit:
            index = index + step
    return index


def one_hot(shape, source):
    row = lax.broadcasted_iota(jnp.int32, (shape[0], 1), 0)
    col = lax.broadcasted_iota(jnp.int32, shape, 1)
    return jnp.where(source(row) == col, 1.0, 0.0).astype(BF16)


def flat(block):
    return block.astype(F32).reshape(-1, block.shape[-1]).astype(BF16)


def layer_kernel(
    slots,
    spread,
    x,
    *refs,
):
    scales, sources, out = refs[:4], refs[4:12], refs[12]
    norms, held, xv, res, q, k, v, a, nsem, wsem, lsem, s1, r1, s2, r2, s3, r3 = refs[13:30]
    chunks = [(h, sum(plan[:n]), few) for h, plan in enumerate(PLAN) for n, few in enumerate(plan)]
    count = len(chunks)
    xs, xt, snd, rcv = [refs[30 + n * count : 30 + (n + 1) * count] for n in range(4)]
    me_t, me_s = lax.axis_index("tm"), lax.axis_index("space")
    halves, rows, _, piece, width = xv.shape
    frames = rows * slots
    peers = slots * spread
    chips = spread // 2
    tokens = frames * piece
    me_c = me_s % 2
    me_z = me_s // 2
    steps_t, steps_s = bit_steps(me_t, slots), bit_steps(me_s, spread)
    steps_z = bit_steps(me_z, chips)

    halves_in = [pltpu.make_async_copy(x.at[:, :, h], xv.at[h], lsem.at[h]) for h in range(halves)]
    loads = [pltpu.make_async_copy(w, held.at[i], wsem.at[i]) for i, w in enumerate(sources)]
    norms_in = [pltpu.make_async_copy(n, norms.at[i], nsem.at[i]) for i, n in enumerate(scales)]
    halves_in[0].start()
    barrier = pltpu.get_barrier_semaphore()
    for mask in range(1, peers):
        pl.semaphore_signal(
            barrier,
            inc=1,
            device_id={
                "tm": moved(me_t, steps_t, mask % slots),
                "space": moved(me_s, steps_s, mask // slots),
            },
        )
    for copy in halves_in[1:] + norms_in + loads:
        copy.start()

    def first(c, mask):
        t = moved(me_t, steps_t, mask)
        return pltpu.make_async_remote_copy(
            src_ref=xs[c].at[t],
            dst_ref=xt[c].at[pl.ds(me_t * rows * chunks[c][2], rows * chunks[c][2])],
            send_sem=s1.at[c],
            recv_sem=r1.at[c],
            device_id={"tm": t},
        )

    def first_all(c):
        part = xt[c].at[pl.ds(0, (slots - 1) * rows * chunks[c][2])]
        return pltpu.make_async_remote_copy(
            src_ref=part,
            dst_ref=part,
            send_sem=s1.at[c],
            recv_sem=r1.at[c],
            device_id={"tm": moved(me_t, steps_t, 1)},
        )

    def second(c, mask, core):
        t, z = moved(me_t, steps_t, mask % slots), moved(me_z, steps_z, mask // slots)
        return pltpu.make_async_remote_copy(
            src_ref=snd[c].at[(t * chips + z) * 2 + core],
            dst_ref=rcv[c].at[me_s * slots + me_t],
            send_sem=s2.at[c],
            recv_sem=r2.at[c],
            device_id={"tm": t, "space": z * 2 + core},
        )

    def second_all(c):
        part = rcv[c].at[pl.ds(0, peers - 1)]
        return pltpu.make_async_remote_copy(
            src_ref=part,
            dst_ref=part,
            send_sem=s2.at[c],
            recv_sem=r2.at[c],
            device_id={"space": me_s + 1 - 2 * me_c},
        )

    def home(h):
        def source(r):
            found = r
            for own, first_place, few in chunks:
                if own == h:
                    start, block = first_place * slots * rows, rows * few
                    n = r - start
                    place = first_place + n % few
                    row = (((n // few) % rows) * slots + (n // block) % slots) * piece + place
                    found = jnp.where(r >= start, row, found)
            return found

        return one_hot((rows * slots * piece,) * 2, source)

    same, folding = {}, {}
    first_home = home(0)
    for few in sorted({few for _, _, few in chunks}):
        size, fold = frames * few, piece // few
        same[few] = (
            lax.broadcasted_iota(jnp.int32, (size, 1), 0) % few
            == lax.broadcasted_iota(jnp.int32, (1, size), 1) % few
        )
        folding[few] = one_hot(
            (fold * size,) * 2,
            lambda r: ((r // few) % fold) * size + (r // piece) * few + r % few,
        )

    for h in range(halves):
        halves_in[h].wait()
        moved_in = project(first_home if h == 0 else home(h), flat(xv[h])).astype(BF16)
        for c, (own, first_place, few) in enumerate(chunks):
            if own == h:
                block = rows * few
                for t in range(slots):
                    start = first_place * slots * rows + t * block
                    xs[c][t] = moved_in[start : start + block]
                xt[c][pl.ds(me_t * block, block)] = xs[c][me_t]
        if h == 0:
            pl.semaphore_wait(barrier, peers - 1)
        for c, (own, _, _) in enumerate(chunks):
            if own == h:
                for mask in range(slots - 1, 0, -1):
                    first(c, mask).start()

    weights = [held.at[i] for i in range(8)]
    waits = [copy.wait for copy in loads]
    for copy in norms_in:
        copy.wait()
    tg, ts, sg, ss = [norms.at[i] for i in range(4)]
    def send(c, core, masks):
        for mask in masks:
            second(c, mask, core).start()

    everyone = list(range(slots * chips - 1, 0, -1))
    for c, (_, _, few) in enumerate(chunks):
        first_all(c).wait_recv()
        size, fold = frames * few, piece // few
        part, columns = pl.ds(0, size), width // fold
        tok = xt[c][...]
        qkv(
            layer_norm(tok, tg[...], ts[...]),
            weights[:3],
            waits[:3] if c == 0 else [lambda: None] * 3,
            [ref.at[part] for ref in (q, k, v)],
        )

        def time_pair(index, carry):
            cols = pl.ds(pl.multiple_of(index * LANES, LANES), LANES)
            a[part, cols] = attend(q[part, cols], k[part, cols], v[part, cols], same[few])
            return carry

        lax.fori_loop(0, width // LANES, time_pair, 0, unroll=UNROLL_T)
        if c == 0:
            waits[3]()
        after = (tok.astype(F32) + project(a[part], weights[3][...])).astype(BF16)
        after = jnp.concatenate([after[:, n * columns : (n + 1) * columns] for n in range(fold)], 0)
        if fold > 1:
            after = project(folding[few], after)
        snd[c][...] = after.astype(F32).reshape(frames, piece, columns).astype(BF16)
        send(c, 0, everyone)
        pltpu.make_async_remote_copy(
            src_ref=snd[c].at[(me_t * chips + me_z) * 2 + 1 - me_c],
            dst_ref=rcv[c].at[me_s * slots + me_t],
            send_sem=s2.at[c],
            recv_sem=r2.at[c],
            device_id={"space": me_z * 2 + 1 - me_c},
        ).start()
        send(c, 1, everyone[: EARLY[c]])
        rcv[c][me_s * slots + me_t] = snd[c][me_t * rows + me_s]
    for c in range(count):
        send(c, 1, everyone[EARLY[c] :])

    for h in range(halves):
        mine = [(c, first_place, few) for c, (own, first_place, few) in enumerate(chunks) if own == h]
        for c, _, _ in mine:
            second_all(c).wait_recv()
        arrived = [(flat(rcv[c][...]), first_place, few) for c, first_place, few in mine]
        finest = max(piece // few for _, _, few in arrived)
        columns = width // finest
        parts = []
        for n in range(finest):
            def source(r):
                place, found = r % piece, r
                for m, (_, first_place, few) in enumerate(arrived):
                    part = n * piece // (finest * few)
                    row = m * tokens + (r // piece) * piece + part * few + place - first_place
                    found = jnp.where(place >= first_place, row, found)
                return found

            stack = []
            for block, _, few in arrived:
                start = (n % (finest * few // piece)) * columns
                stack.append(block[:, start : start + columns])
            hot = one_hot((tokens, len(arrived) * tokens), source)
            parts.append(project(hot, jnp.concatenate(stack, 0)).astype(BF16))
        frame = jnp.concatenate(parts, 1)
        res[:, :, h] = frame.astype(F32).reshape(spread, slots, piece, width).astype(BF16)
        qkv(
            layer_norm(frame, sg[...], ss[...]),
            weights[4:7],
            waits[4:7] if h == 0 else [lambda: None] * 3,
            [ref.at[pl.ds(h * tokens, tokens)] for ref in (q, k, v)],
        )
    waits[7]()
    share = slots * piece
    both = 2 * share

    def third(target):
        return pltpu.make_async_remote_copy(
            src_ref=res.at[target],
            dst_ref=out.at[me_s],
            send_sem=s3,
            recv_sem=r3,
            device_id={"space": target},
        )

    near = chips // 2
    targets = [(1 - me_z // near) * near + n for n in range(near)] if near else []
    targets += [moved(me_z, steps_z, mask) for mask in range(near - 1, 0, -1)]
    for target in targets + [me_z]:
        parts = [
            pl.ds(pl.multiple_of(h * tokens + target * both, both), both) for h in range(halves)
        ]

        def attend_pair(index, carry):
            cols = pl.ds(pl.multiple_of(index * LANES, LANES), LANES)
            queries = jnp.concatenate([q[part, cols] for part in parts], 0)
            result = attend(queries, k[:, cols], v[:, cols], None)
            for h, part in enumerate(parts):
                a[part, cols] = result[h * both : (h + 1) * both]
            return carry

        lax.fori_loop(0, width // LANES, attend_pair, 0, unroll=UNROLL_S)
        added = project(jnp.concatenate([a[part] for part in parts], 0), weights[7][...])
        here = pl.ds(2 * target, 2)
        for h in range(halves):
            new = added[h * both : (h + 1) * both].reshape(2, slots, piece, width)
            res[here, :, h] = (res[here, :, h].astype(F32) + new).astype(BF16)
        if target is me_z:
            third(me_s + 1 - 2 * me_c).start()
        else:
            for core in (1, 0):
                third(2 * target + core).start()
    last = pltpu.make_async_copy(res.at[me_s], out.at[me_s], lsem.at[0])
    last.start()
    for c in range(count):
        first_all(c).wait_send()
        second_all(c).wait_send()
    others = pl.ds(0, spread - 1)
    pltpu.make_async_remote_copy(
        src_ref=res.at[others],
        dst_ref=out.at[others],
        send_sem=s3,
        recv_sem=r3,
        device_id={"space": me_s + 1 - 2 * me_c},
    ).wait()
    last.wait()


def run_layer(frames_in, slots, spread, norms, weights):
    rows, patches, width = frames_in.shape
    frames, places, halves = rows * slots, patches // slots, 2
    piece = places // halves
    total = frames * places
    fews = [few for plan in PLAN for few in plan]
    vmem, hbm = pl.BlockSpec(memory_space=pltpu.VMEM), pl.BlockSpec(memory_space=pltpu.HBM)
    dma = pltpu.SemaphoreType.DMA
    return pl.pallas_call(
        functools.partial(layer_kernel, slots, spread),
        out_shape=pltpu.VMEM((rows, slots, halves, piece, width), BF16),
        in_specs=[hbm] * 13,
        out_specs=vmem,
        scratch_shapes=[
            pltpu.VMEM((4, 1, width), F32),
            pltpu.VMEM((8, width, width), BF16),
            pltpu.VMEM((halves, rows, slots, piece, width), BF16),
            pltpu.VMEM((spread, slots, halves, piece, width), BF16),
        ]
        + [pltpu.VMEM((total, width), BF16)] * 4
        + [
            dma((4,)),
            dma((8,)),
            dma((halves,)),
            dma((len(fews),)),
            dma((len(fews),)),
            dma((len(fews),)),
            dma((len(fews),)),
            dma(()),
            dma(()),
        ]
        + [pltpu.VMEM((slots, rows * few, width), BF16) for few in fews]
        + [pltpu.VMEM((frames * few, width), BF16) for few in fews]
        + [pltpu.VMEM((frames, piece, width * few // piece), BF16) for few in fews]
        + [pltpu.VMEM((slots * spread, piece, width * few // piece), BF16) for few in fews],
        compiler_params=pltpu.CompilerParams(
            collective_id=0, has_side_effects=True, vmem_limit_bytes=60 << 20
        ),
    )(
        frames_in.reshape(rows, slots, halves, piece, width),
        *[norm.reshape(1, -1) for norm in norms],
        *weights,
    ).reshape(frames_in.shape)


def split_heads(tokens):
    return tokens.reshape(tokens.shape[0], tokens.shape[1], tokens.shape[2] // HEAD_DIM, HEAD_DIM)


def gathered_space(after_time, gain, shift, wq, wk, wv, wo):
    normed = layer_norm(after_time, gain, shift)
    queries = project(normed, wq).astype(BF16)
    everywhere = lax.all_gather(normed, "space", axis=1, tiled=True)
    keys_in, values_in = (project(everywhere, w).astype(BF16) for w in (wk, wv))
    scores = 0.125 * jnp.einsum(
        "fqhd,fkhd->fhqk", split_heads(queries), split_heads(keys_in), preferred_element_type=F32
    )
    weights = jax.nn.softmax(scores, axis=-1).astype(BF16)
    spatial = jnp.einsum(
        "fhqk,fkhd->fqhd", weights, split_heads(values_in), preferred_element_type=F32
    )
    spatial = spatial.astype(BF16).reshape(after_time.shape)
    return (after_time.astype(F32) + project(spatial, wo)).astype(BF16)


def body(frames_in, tg, ts, tq, tk, tv, to, sg, ss, sq, sk, sv, so):
    slots, spread = lax.axis_size("tm"), lax.axis_size("space")
    rows, patches, width = frames_in.shape
    frames, places = rows * slots, patches // slots
    powers = not (slots & (slots - 1) or spread & (spread - 1)) and spread % 2 == 0
    tiles = places == 16 and width % (4 * LANES) == 0
    if rows == spread and powers and tiles:
        return run_layer(
            frames_in, slots, spread, (tg, ts, sg, ss), (tq, tk, tv, to, sq, sk, sv, so)
        )
    tokens = lax.all_to_all(
        frames_in.reshape(rows, slots, places, width), "tm", split_axis=1, concat_axis=0, tiled=True
    ).reshape(frames * places, width)
    after = run_branch(functools.partial(time_branch, frames), tokens, tg, ts, tq, tk, tv, to)
    after = lax.all_to_all(
        after.reshape(frames, 1, places, width), "tm", split_axis=0, concat_axis=1, tiled=True
    ).reshape(rows, patches, width)
    return gathered_space(after, sg, ss, sq, sk, sv, so)


def solution(mesh):
    return jax.shard_map(
        body,
        mesh=mesh,
        in_specs=(P("tm", "space", None),) + (P(),) * 12,
        out_specs=P("tm", "space", None),
        check_vma=False,
    )
```

```python
import functools
import math

import jax
import jax.numpy as jnp
from jax import lax
from jax.experimental import pallas as pl
from jax.experimental.pallas import tpu as pltpu
from jax.sharding import PartitionSpec as P

HEAD_DIM = 64
LANES = 128
UNROLL_T, UNROLL_S = 8, 8
PLAN = ((2, 2, 4), (4, 4))
EARLY = (7, 7, 2, 0, 0)
SCALE = 0.125 * math.log2(math.e)
F32, BF16 = jnp.float32, jnp.bfloat16


def layer_norm(tokens, gain, shift):
    values = tokens.astype(F32)
    mean_value = jnp.mean(values, axis=-1, keepdims=True)
    centred = values - mean_value
    variance = jnp.mean(centred * centred, axis=-1, keepdims=True)
    return (centred * lax.rsqrt(variance + 1e-05) * gain + shift).astype(BF16)


def project(tokens, weight):
    return jnp.dot(tokens, weight, preferred_element_type=F32)


def permutation(rows, inner, outer, back):
    row = lax.broadcasted_iota(jnp.int32, (rows, rows), 1 if back else 0)
    col = lax.broadcasted_iota(jnp.int32, (rows, rows), 0 if back else 1)
    return jnp.where((row % inner) * outer + row // inner == col, 1.0, 0.0).astype(BF16)


def lane_masks(width):
    lane = lax.broadcasted_iota(jnp.int32, (1, LANES), 1)
    return [(lane // HEAD_DIM == part) for part in range(LANES // HEAD_DIM)]


def attend(queries, keys_in, values_in, same):
    rows = queries.shape[0]
    masks = lane_masks(LANES)
    own = jnp.concatenate([jnp.where(mask, queries, jnp.zeros_like(queries)) for mask in masks], 0)
    scores = lax.dot_general(own, keys_in, (((1,), (1,)), ((), ())), preferred_element_type=F32)
    if same is not None:
        scores = jnp.where(jnp.concatenate([same] * len(masks), 0), scores, -1e30)
    top = jnp.max(scores, axis=-1, keepdims=True)
    weights = jnp.exp2((scores - top) * SCALE).astype(BF16)
    both = jnp.concatenate([values_in, jnp.ones_like(values_in)], 1)
    added = jnp.dot(weights, both, preferred_element_type=F32)
    added = added[:, :LANES] / added[:, LANES:]
    result = added[:rows]
    for part in range(1, len(masks)):
        result = jnp.where(masks[part], added[part * rows : (part + 1) * rows], result)
    return result.astype(BF16)


def qkv(normed, weights, waits, outs):
    for weight, wait, out in zip(weights, waits, outs):
        wait()
        out[...] = project(normed, weight[...]).astype(BF16)


def time_branch(frames, x, gain, shift, weights, waits, q, k, v, a):
    rows, width = q.shape
    places = rows // frames
    order = permutation(rows, frames, places, False)
    x = project(order, x).astype(BF16)
    qkv(layer_norm(x, gain, shift), weights[:3], waits[:3], (q, k, v))
    size = max(frames, LANES)
    same = (
        lax.broadcasted_iota(jnp.int32, (size, size), 0) // frames
        == lax.broadcasted_iota(jnp.int32, (size, size), 1) // frames
    )

    def pair(index, carry):
        cols = pl.ds(pl.multiple_of(index * LANES, LANES), LANES)
        for group in range(rows // size):
            part = (pl.ds(group * size, size), cols)
            a[part] = attend(q[part], k[part], v[part], same)
        return carry

    lax.fori_loop(0, width // LANES, pair, 0, unroll=UNROLL_T)
    waits[3]()
    after = (x.astype(F32) + project(a[...], weights[3][...])).astype(BF16)
    return project(permutation(rows, frames, places, True), after)


def branch_kernel(branch, x, gain, shift, w0, w1, w2, w3, out, held, q, k, v, a, sems):
    copies = [
        pltpu.make_async_copy(w, held.at[i], sems.at[i]) for i, w in enumerate((w0, w1, w2, w3))
    ]
    for copy in copies:
        copy.start()
    weights = [held.at[i] for i in range(4)]
    waits = [copy.wait for copy in copies]
    out[...] = branch(x[...], gain[...], shift[...], weights, waits, q, k, v, a).astype(BF16)


def run_branch(branch, x, gain, shift, *weights):
    rows, width = x.shape
    vmem = pl.BlockSpec(memory_space=pltpu.VMEM)
    return pl.pallas_call(
        functools.partial(branch_kernel, branch),
        out_shape=jax.ShapeDtypeStruct((rows, width), BF16),
        in_specs=[vmem] * 3 + [pl.BlockSpec(memory_space=pl.ANY)] * 4,
        out_specs=vmem,
        scratch_shapes=[pltpu.VMEM((4, width, width), BF16)]
        + [pltpu.VMEM((rows, width), BF16)] * 4
        + [pltpu.SemaphoreType.DMA((4,))],
        compiler_params=pltpu.CompilerParams(vmem_limit_bytes=60 << 20),
    )(x, gain.reshape(1, -1), shift.reshape(1, -1), *weights)


def bit_steps(index, count):
    out, bit = [], 1
    while bit < count:
        out.append((bit, bit - 2 * bit * ((index // bit) % 2)))
        bit *= 2
    return out


def moved(index, steps, mask):
    for bit, step in steps:
        if mask & bit:
            index = index + step
    return index


def one_hot(shape, source):
    row = lax.broadcasted_iota(jnp.int32, (shape[0], 1), 0)
    col = lax.broadcasted_iota(jnp.int32, shape, 1)
    return jnp.where(source(row) == col, 1.0, 0.0).astype(BF16)


def flat(block):
    return block.astype(F32).reshape(-1, block.shape[-1]).astype(BF16)


def layer_kernel(
    slots,
    spread,
    x,
    *refs,
):
    scales, sources, out = refs[:4], refs[4:12], refs[12]
    norms, held, xv, res, q, k, v, a, nsem, wsem, lsem, s1, r1, s2, r2, s3, r3 = refs[13:30]
    chunks = [(h, sum(plan[:n]), few) for h, plan in enumerate(PLAN) for n, few in enumerate(plan)]
    count = len(chunks)
    xs, xt, snd, rcv = [refs[30 + n * count : 30 + (n + 1) * count] for n in range(4)]
    me_t, me_s = lax.axis_index("tm"), lax.axis_index("space")
    halves, rows, _, piece, width = xv.shape
    frames = rows * slots
    peers = slots * spread
    chips = spread // 2
    tokens = frames * piece
    me_c = me_s % 2
    me_z = me_s // 2
    steps_t, steps_s = bit_steps(me_t, slots), bit_steps(me_s, spread)
    steps_z = bit_steps(me_z, chips)

    halves_in = [pltpu.make_async_copy(x.at[:, :, h], xv.at[h], lsem.at[h]) for h in range(halves)]
    loads = [pltpu.make_async_copy(w, held.at[i], wsem.at[i]) for i, w in enumerate(sources)]
    norms_in = [pltpu.make_async_copy(n, norms.at[i], nsem.at[i]) for i, n in enumerate(scales)]
    halves_in[0].start()
    barrier = pltpu.get_barrier_semaphore()
    for mask in range(1, peers):
        pl.semaphore_signal(
            barrier,
            inc=1,
            device_id={
                "tm": moved(me_t, steps_t, mask % slots),
                "space": moved(me_s, steps_s, mask // slots),
            },
        )
    for copy in halves_in[1:] + norms_in + loads:
        copy.start()

    def first(c, mask):
        t = moved(me_t, steps_t, mask)
        return pltpu.make_async_remote_copy(
            src_ref=xs[c].at[t],
            dst_ref=xt[c].at[pl.ds(me_t * rows * chunks[c][2], rows * chunks[c][2])],
            send_sem=s1.at[c],
            recv_sem=r1.at[c],
            device_id={"tm": t},
        )

    def first_all(c):
        part = xt[c].at[pl.ds(0, (slots - 1) * rows * chunks[c][2])]
        return pltpu.make_async_remote_copy(
            src_ref=part,
            dst_ref=part,
            send_sem=s1.at[c],
            recv_sem=r1.at[c],
            device_id={"tm": moved(me_t, steps_t, 1)},
        )

    def second(c, mask, core):
        t, z = moved(me_t, steps_t, mask % slots), moved(me_z, steps_z, mask // slots)
        return pltpu.make_async_remote_copy(
            src_ref=snd[c].at[(t * chips + z) * 2 + core],
            dst_ref=rcv[c].at[me_s * slots + me_t],
            send_sem=s2.at[c],
            recv_sem=r2.at[c],
            device_id={"tm": t, "space": z * 2 + core},
        )

    def second_all(c):
        part = rcv[c].at[pl.ds(0, peers - 1)]
        return pltpu.make_async_remote_copy(
            src_ref=part,
            dst_ref=part,
            send_sem=s2.at[c],
            recv_sem=r2.at[c],
            device_id={"space": me_s + 1 - 2 * me_c},
        )

    def home(h):
        def source(r):
            found = r
            for own, first_place, few in chunks:
                if own == h:
                    start, block = first_place * slots * rows, rows * few
                    n = r - start
                    place = first_place + n % few
                    row = (((n // few) % rows) * slots + (n // block) % slots) * piece + place
                    found = jnp.where(r >= start, row, found)
            return found

        return one_hot((rows * slots * piece,) * 2, source)

    same, folding = {}, {}
    first_home = home(0)
    for few in sorted({few for _, _, few in chunks}):
        size, fold = frames * few, piece // few
        same[few] = (
            lax.broadcasted_iota(jnp.int32, (size, 1), 0) % few
            == lax.broadcasted_iota(jnp.int32, (1, size), 1) % few
        )
        folding[few] = one_hot(
            (fold * size,) * 2,
            lambda r: ((r // few) % fold) * size + (r // piece) * few + r % few,
        )

    for h in range(halves):
        halves_in[h].wait()
        moved_in = project(first_home if h == 0 else home(h), flat(xv[h])).astype(BF16)
        for c, (own, first_place, few) in enumerate(chunks):
            if own == h:
                block = rows * few
                for t in range(slots):
                    start = first_place * slots * rows + t * block
                    xs[c][t] = moved_in[start : start + block]
                xt[c][pl.ds(me_t * block, block)] = xs[c][me_t]
        if h == 0:
            pl.semaphore_wait(barrier, peers - 1)
        for c, (own, _, _) in enumerate(chunks):
            if own == h:
                for mask in range(slots - 1, 0, -1):
                    first(c, mask).start()

    weights = [held.at[i] for i in range(8)]
    waits = [copy.wait for copy in loads]
    for copy in norms_in:
        copy.wait()
    tg, ts, sg, ss = [norms.at[i] for i in range(4)]
    def send(c, core, masks):
        for mask in masks:
            second(c, mask, core).start()

    everyone = list(range(slots * chips - 1, 0, -1))
    for c, (_, _, few) in enumerate(chunks):
        first_all(c).wait_recv()
        size, fold = frames * few, piece // few
        part, columns = pl.ds(0, size), width // fold
        tok = xt[c][...]
        qkv(
            layer_norm(tok, tg[...], ts[...]),
            weights[:3],
            waits[:3] if c == 0 else [lambda: None] * 3,
            [ref.at[part] for ref in (q, k, v)],
        )

        def time_pair(index, carry):
            cols = pl.ds(pl.multiple_of(index * LANES, LANES), LANES)
            a[part, cols] = attend(q[part, cols], k[part, cols], v[part, cols], same[few])
            return carry

        lax.fori_loop(0, width // LANES, time_pair, 0, unroll=UNROLL_T)
        if c == 0:
            waits[3]()
        after = (tok.astype(F32) + project(a[part], weights[3][...])).astype(BF16)
        after = jnp.concatenate([after[:, n * columns : (n + 1) * columns] for n in range(fold)], 0)
        if fold > 1:
            after = project(folding[few], after)
        snd[c][...] = after.astype(F32).reshape(frames, piece, columns).astype(BF16)
        send(c, 0, everyone)
        pltpu.make_async_remote_copy(
            src_ref=snd[c].at[(me_t * chips + me_z) * 2 + 1 - me_c],
            dst_ref=rcv[c].at[me_s * slots + me_t],
            send_sem=s2.at[c],
            recv_sem=r2.at[c],
            device_id={"space": me_z * 2 + 1 - me_c},
        ).start()
        send(c, 1, everyone[: EARLY[c]])
        rcv[c][me_s * slots + me_t] = snd[c][me_t * rows + me_s]
    for c in range(count):
        send(c, 1, everyone[EARLY[c] :])

    for h in range(halves):
        mine = [(c, first_place, few) for c, (own, first_place, few) in enumerate(chunks) if own == h]
        for c, _, _ in mine:
            second_all(c).wait_recv()
        arrived = [(flat(rcv[c][...]), first_place, few) for c, first_place, few in mine]
        finest = max(piece // few for _, _, few in arrived)
        columns = width // finest
        parts = []
        for n in range(finest):
            def source(r):
                place, found = r % piece, r
                for m, (_, first_place, few) in enumerate(arrived):
                    part = n * piece // (finest * few)
                    row = m * tokens + (r // piece) * piece + part * few + place - first_place
                    found = jnp.where(place >= first_place, row, found)
                return found

            stack = []
            for block, _, few in arrived:
                start = (n % (finest * few // piece)) * columns
                stack.append(block[:, start : start + columns])
            hot = one_hot((tokens, len(arrived) * tokens), source)
            parts.append(project(hot, jnp.concatenate(stack, 0)).astype(BF16))
        frame = jnp.concatenate(parts, 1)
        res[:, :, h] = frame.astype(F32).reshape(spread, slots, piece, width).astype(BF16)
        qkv(
            layer_norm(frame, sg[...], ss[...]),
            weights[4:7],
            waits[4:7] if h == 0 else [lambda: None] * 3,
            [ref.at[pl.ds(h * tokens, tokens)] for ref in (q, k, v)],
        )
    waits[7]()
    share = slots * piece
    both = 2 * share

    def third(target):
        return pltpu.make_async_remote_copy(
            src_ref=res.at[target],
            dst_ref=out.at[me_s],
            send_sem=s3,
            recv_sem=r3,
            device_id={"space": target},
        )

    near = chips // 2
    targets = [(1 - me_z // near) * near + n for n in range(near)] if near else []
    targets += [moved(me_z, steps_z, mask) for mask in range(near - 1, 0, -1)]
    for target in targets + [me_z]:
        parts = [
            pl.ds(pl.multiple_of(h * tokens + target * both, both), both) for h in range(halves)
        ]

        def attend_pair(index, carry):
            cols = pl.ds(pl.multiple_of(index * LANES, LANES), LANES)
            queries = jnp.concatenate([q[part, cols] for part in parts], 0)
            result = attend(queries, k[:, cols], v[:, cols], None)
            for h, part in enumerate(parts):
                a[part, cols] = result[h * both : (h + 1) * both]
            return carry

        lax.fori_loop(0, width // LANES, attend_pair, 0, unroll=UNROLL_S)
        added = project(jnp.concatenate([a[part] for part in parts], 0), weights[7][...])
        here = pl.ds(2 * target, 2)
        for h in range(halves):
            new = added[h * both : (h + 1) * both].reshape(2, slots, piece, width)
            res[here, :, h] = (res[here, :, h].astype(F32) + new).astype(BF16)
        if target is me_z:
            third(me_s + 1 - 2 * me_c).start()
        else:
            for core in (1, 0):
                third(2 * target + core).start()
    last = pltpu.make_async_copy(res.at[me_s], out.at[me_s], lsem.at[0])
    last.start()
    for c in range(count):
        first_all(c).wait_send()
        second_all(c).wait_send()
    others = pl.ds(0, spread - 1)
    pltpu.make_async_remote_copy(
        src_ref=res.at[others],
        dst_ref=out.at[others],
        send_sem=s3,
        recv_sem=r3,
        device_id={"space": me_s + 1 - 2 * me_c},
    ).wait()
    last.wait()


def run_layer(frames_in, slots, spread, norms, weights):
    rows, patches, width = frames_in.shape
    frames, places, halves = rows * slots, patches // slots, 2
    piece = places // halves
    total = frames * places
    fews = [few for plan in PLAN for few in plan]
    vmem, hbm = pl.BlockSpec(memory_space=pltpu.VMEM), pl.BlockSpec(memory_space=pltpu.HBM)
    dma = pltpu.SemaphoreType.DMA
    return pl.pallas_call(
        functools.partial(layer_kernel, slots, spread),
        out_shape=pltpu.VMEM((rows, slots, halves, piece, width), BF16),
        in_specs=[hbm] * 13,
        out_specs=vmem,
        scratch_shapes=[
            pltpu.VMEM((4, 1, width), F32),
            pltpu.VMEM((8, width, width), BF16),
            pltpu.VMEM((halves, rows, slots, piece, width), BF16),
            pltpu.VMEM((spread, slots, halves, piece, width), BF16),
        ]
        + [pltpu.VMEM((total, width), BF16)] * 4
        + [
            dma((4,)),
            dma((8,)),
            dma((halves,)),
            dma((len(fews),)),
            dma((len(fews),)),
            dma((len(fews),)),
            dma((len(fews),)),
            dma(()),
            dma(()),
        ]
        + [pltpu.VMEM((slots, rows * few, width), BF16) for few in fews]
        + [pltpu.VMEM((frames * few, width), BF16) for few in fews]
        + [pltpu.VMEM((frames, piece, width * few // piece), BF16) for few in fews]
        + [pltpu.VMEM((slots * spread, piece, width * few // piece), BF16) for few in fews],
        compiler_params=pltpu.CompilerParams(
            collective_id=0, has_side_effects=True, vmem_limit_bytes=60 << 20
        ),
    )(
        frames_in.reshape(rows, slots, halves, piece, width),
        *[norm.reshape(1, -1) for norm in norms],
        *weights,
    ).reshape(frames_in.shape)


def split_heads(tokens):
    return tokens.reshape(tokens.shape[0], tokens.shape[1], tokens.shape[2] // HEAD_DIM, HEAD_DIM)


def gathered_space(after_time, gain, shift, wq, wk, wv, wo):
    normed = layer_norm(after_time, gain, shift)
    queries = project(normed, wq).astype(BF16)
    everywhere = lax.all_gather(normed, "space", axis=1, tiled=True)
    keys_in, values_in = (project(everywhere, w).astype(BF16) for w in (wk, wv))
    scores = 0.125 * jnp.einsum(
        "fqhd,fkhd->fhqk", split_heads(queries), split_heads(keys_in), preferred_element_type=F32
    )
    weights = jax.nn.softmax(scores, axis=-1).astype(BF16)
    spatial = jnp.einsum(
        "fhqk,fkhd->fqhd", weights, split_heads(values_in), preferred_element_type=F32
    )
    spatial = spatial.astype(BF16).reshape(after_time.shape)
    return (after_time.astype(F32) + project(spatial, wo)).astype(BF16)


def body(frames_in, tg, ts, tq, tk, tv, to, sg, ss, sq, sk, sv, so):
    slots, spread = lax.axis_size("tm"), lax.axis_size("space")
    rows, patches, width = frames_in.shape
    frames, places = rows * slots, patches // slots
    powers = not (slots & (slots - 1) or spread & (spread - 1)) and spread % 2 == 0
    tiles = places == 16 and width % (4 * LANES) == 0
    if rows == spread and powers and tiles:
        return run_layer(
            frames_in, slots, spread, (tg, ts, sg, ss), (tq, tk, tv, to, sq, sk, sv, so)
        )
    tokens = lax.all_to_all(
        frames_in.reshape(rows, slots, places, width), "tm", split_axis=1, concat_axis=0, tiled=True
    ).reshape(frames * places, width)
    after = run_branch(functools.partial(time_branch, frames), tokens, tg, ts, tq, tk, tv, to)
    after = lax.all_to_all(
        after.reshape(frames, 1, places, width), "tm", split_axis=0, concat_axis=1, tiled=True
    ).reshape(rows, patches, width)
    return gathered_space(after, sg, ss, sq, sk, sv, so)


def solution(mesh):
    return jax.shard_map(
        body,
        mesh=mesh,
        in_specs=(P("tm", "space", None),) + (P(),) * 12,
        out_specs=P("tm", "space", None),
        check_vma=False,
    )
```

```python
import functools
import math

import jax
import jax.numpy as jnp
from jax import lax
from jax.experimental import pallas as pl
from jax.experimental.pallas import tpu as pltpu
from jax.sharding import PartitionSpec as P

HEAD_DIM = 64
LANES = 128
UNROLL_T, UNROLL_S = 8, 8
PLAN = ((2, 2, 4), (4, 4))
EARLY = (7, 7, 2, 0, 0)
SCALE = 0.125 * math.log2(math.e)
F32, BF16 = jnp.float32, jnp.bfloat16


def layer_norm(tokens, gain, shift):
    values = tokens.astype(F32)
    mean_value = jnp.mean(values, axis=-1, keepdims=True)
    centred = values - mean_value
    variance = jnp.mean(centred * centred, axis=-1, keepdims=True)
    return (centred * lax.rsqrt(variance + 1e-05) * gain + shift).astype(BF16)


def project(tokens, weight):
    return jnp.dot(tokens, weight, preferred_element_type=F32)


def permutation(rows, inner, outer, back):
    row = lax.broadcasted_iota(jnp.int32, (rows, rows), 1 if back else 0)
    col = lax.broadcasted_iota(jnp.int32, (rows, rows), 0 if back else 1)
    return jnp.where((row % inner) * outer + row // inner == col, 1.0, 0.0).astype(BF16)


def lane_masks(width):
    lane = lax.broadcasted_iota(jnp.int32, (1, LANES), 1)
    return [(lane // HEAD_DIM == part) for part in range(LANES // HEAD_DIM)]


def attend(queries, keys_in, values_in, same):
    rows = queries.shape[0]
    masks = lane_masks(LANES)
    own = jnp.concatenate([jnp.where(mask, queries, jnp.zeros_like(queries)) for mask in masks], 0)
    scores = lax.dot_general(own, keys_in, (((1,), (1,)), ((), ())), preferred_element_type=F32)
    if same is not None:
        scores = jnp.where(jnp.concatenate([same] * len(masks), 0), scores, -1e30)
    top = jnp.max(scores, axis=-1, keepdims=True)
    weights = jnp.exp2((scores - top) * SCALE).astype(BF16)
    both = jnp.concatenate([values_in, jnp.ones_like(values_in)], 1)
    added = jnp.dot(weights, both, preferred_element_type=F32)
    added = added[:, :LANES] / added[:, LANES:]
    result = added[:rows]
    for part in range(1, len(masks)):
        result = jnp.where(masks[part], added[part * rows : (part + 1) * rows], result)
    return result.astype(BF16)


def qkv(normed, weights, waits, outs):
    for weight, wait, out in zip(weights, waits, outs):
        wait()
        out[...] = project(normed, weight[...]).astype(BF16)


def time_branch(frames, x, gain, shift, weights, waits, q, k, v, a):
    rows, width = q.shape
    places = rows // frames
    order = permutation(rows, frames, places, False)
    x = project(order, x).astype(BF16)
    qkv(layer_norm(x, gain, shift), weights[:3], waits[:3], (q, k, v))
    size = max(frames, LANES)
    same = (
        lax.broadcasted_iota(jnp.int32, (size, size), 0) // frames
        == lax.broadcasted_iota(jnp.int32, (size, size), 1) // frames
    )

    def pair(index, carry):
        cols = pl.ds(pl.multiple_of(index * LANES, LANES), LANES)
        for group in range(rows // size):
            part = (pl.ds(group * size, size), cols)
            a[part] = attend(q[part], k[part], v[part], same)
        return carry

    lax.fori_loop(0, width // LANES, pair, 0, unroll=UNROLL_T)
    waits[3]()
    after = (x.astype(F32) + project(a[...], weights[3][...])).astype(BF16)
    return project(permutation(rows, frames, places, True), after)


def branch_kernel(branch, x, gain, shift, w0, w1, w2, w3, out, held, q, k, v, a, sems):
    copies = [
        pltpu.make_async_copy(w, held.at[i], sems.at[i]) for i, w in enumerate((w0, w1, w2, w3))
    ]
    for copy in copies:
        copy.start()
    weights = [held.at[i] for i in range(4)]
    waits = [copy.wait for copy in copies]
    out[...] = branch(x[...], gain[...], shift[...], weights, waits, q, k, v, a).astype(BF16)


def run_branch(branch, x, gain, shift, *weights):
    rows, width = x.shape
    vmem = pl.BlockSpec(memory_space=pltpu.VMEM)
    return pl.pallas_call(
        functools.partial(branch_kernel, branch),
        out_shape=jax.ShapeDtypeStruct((rows, width), BF16),
        in_specs=[vmem] * 3 + [pl.BlockSpec(memory_space=pl.ANY)] * 4,
        out_specs=vmem,
        scratch_shapes=[pltpu.VMEM((4, width, width), BF16)]
        + [pltpu.VMEM((rows, width), BF16)] * 4
        + [pltpu.SemaphoreType.DMA((4,))],
        compiler_params=pltpu.CompilerParams(vmem_limit_bytes=60 << 20),
    )(x, gain.reshape(1, -1), shift.reshape(1, -1), *weights)


def bit_steps(index, count):
    out, bit = [], 1
    while bit < count:
        out.append((bit, bit - 2 * bit * ((index // bit) % 2)))
        bit *= 2
    return out


def moved(index, steps, mask):
    for bit, step in steps:
        if mask & bit:
            index = index + step
    return index


def one_hot(shape, source):
    row = lax.broadcasted_iota(jnp.int32, (shape[0], 1), 0)
    col = lax.broadcasted_iota(jnp.int32, shape, 1)
    return jnp.where(source(row) == col, 1.0, 0.0).astype(BF16)


def flat(block):
    return block.astype(F32).reshape(-1, block.shape[-1]).astype(BF16)


def layer_kernel(
    slots,
    spread,
    x,
    *refs,
):
    scales, sources, out = refs[:4], refs[4:12], refs[12]
    norms, held, xv, res, q, k, v, a, nsem, wsem, lsem, s1, r1, s2, r2, s3, r3 = refs[13:30]
    chunks = [(h, sum(plan[:n]), few) for h, plan in enumerate(PLAN) for n, few in enumerate(plan)]
    count = len(chunks)
    xs, xt, snd, rcv = [refs[30 + n * count : 30 + (n + 1) * count] for n in range(4)]
    me_t, me_s = lax.axis_index("tm"), lax.axis_index("space")
    halves, rows, _, piece, width = xv.shape
    frames = rows * slots
    peers = slots * spread
    chips = spread // 2
    tokens = frames * piece
    me_c = me_s % 2
    me_z = me_s // 2
    steps_t, steps_s = bit_steps(me_t, slots), bit_steps(me_s, spread)
    steps_z = bit_steps(me_z, chips)

    halves_in = [pltpu.make_async_copy(x.at[:, :, h], xv.at[h], lsem.at[h]) for h in range(halves)]
    loads = [pltpu.make_async_copy(w, held.at[i], wsem.at[i]) for i, w in enumerate(sources)]
    norms_in = [pltpu.make_async_copy(n, norms.at[i], nsem.at[i]) for i, n in enumerate(scales)]
    halves_in[0].start()
    barrier = pltpu.get_barrier_semaphore()
    for mask in range(1, peers):
        pl.semaphore_signal(
            barrier,
            inc=1,
            device_id={
                "tm": moved(me_t, steps_t, mask % slots),
                "space": moved(me_s, steps_s, mask // slots),
            },
        )
    for copy in halves_in[1:] + norms_in + loads:
        copy.start()

    def first(c, mask):
        t = moved(me_t, steps_t, mask)
        return pltpu.make_async_remote_copy(
            src_ref=xs[c].at[t],
            dst_ref=xt[c].at[pl.ds(me_t * rows * chunks[c][2], rows * chunks[c][2])],
            send_sem=s1.at[c],
            recv_sem=r1.at[c],
            device_id={"tm": t},
        )

    def first_all(c):
        part = xt[c].at[pl.ds(0, (slots - 1) * rows * chunks[c][2])]
        return pltpu.make_async_remote_copy(
            src_ref=part,
            dst_ref=part,
            send_sem=s1.at[c],
            recv_sem=r1.at[c],
            device_id={"tm": moved(me_t, steps_t, 1)},
        )

    def second(c, mask, core):
        t, z = moved(me_t, steps_t, mask % slots), moved(me_z, steps_z, mask // slots)
        return pltpu.make_async_remote_copy(
            src_ref=snd[c].at[(t * chips + z) * 2 + core],
            dst_ref=rcv[c].at[me_s * slots + me_t],
            send_sem=s2.at[c],
            recv_sem=r2.at[c],
            device_id={"tm": t, "space": z * 2 + core},
        )

    def second_all(c):
        part = rcv[c].at[pl.ds(0, peers - 1)]
        return pltpu.make_async_remote_copy(
            src_ref=part,
            dst_ref=part,
            send_sem=s2.at[c],
            recv_sem=r2.at[c],
            device_id={"space": me_s + 1 - 2 * me_c},
        )

    def home(h):
        def source(r):
            found = r
            for own, first_place, few in chunks:
                if own == h:
                    start, block = first_place * slots * rows, rows * few
                    n = r - start
                    place = first_place + n % few
                    row = (((n // few) % rows) * slots + (n // block) % slots) * piece + place
                    found = jnp.where(r >= start, row, found)
            return found

        return one_hot((rows * slots * piece,) * 2, source)

    same, folding = {}, {}
    first_home = home(0)
    for few in sorted({few for _, _, few in chunks}):
        size, fold = frames * few, piece // few
        same[few] = (
            lax.broadcasted_iota(jnp.int32, (size, 1), 0) % few
            == lax.broadcasted_iota(jnp.int32, (1, size), 1) % few
        )
        folding[few] = one_hot(
            (fold * size,) * 2,
            lambda r: ((r // few) % fold) * size + (r // piece) * few + r % few,
        )

    for h in range(halves):
        halves_in[h].wait()
        moved_in = project(first_home if h == 0 else home(h), flat(xv[h])).astype(BF16)
        for c, (own, first_place, few) in enumerate(chunks):
            if own == h:
                block = rows * few
                for t in range(slots):
                    start = first_place * slots * rows + t * block
                    xs[c][t] = moved_in[start : start + block]
                xt[c][pl.ds(me_t * block, block)] = xs[c][me_t]
        if h == 0:
            pl.semaphore_wait(barrier, peers - 1)
        for c, (own, _, _) in enumerate(chunks):
            if own == h:
                for mask in range(slots - 1, 0, -1):
                    first(c, mask).start()

    weights = [held.at[i] for i in range(8)]
    waits = [copy.wait for copy in loads]
    for copy in norms_in:
        copy.wait()
    tg, ts, sg, ss = [norms.at[i] for i in range(4)]
    def send(c, core, masks):
        for mask in masks:
            second(c, mask, core).start()

    everyone = list(range(slots * chips - 1, 0, -1))
    straight = sorted(everyone, key=lambda mask: mask % slots > 0)
    for c, (_, _, few) in enumerate(chunks):
        first_all(c).wait_recv()
        size, fold = frames * few, piece // few
        part, columns = pl.ds(0, size), width // fold
        tok = xt[c][...]
        qkv(
            layer_norm(tok, tg[...], ts[...]),
            weights[:3],
            waits[:3] if c == 0 else [lambda: None] * 3,
            [ref.at[part] for ref in (q, k, v)],
        )

        def time_pair(index, carry):
            cols = pl.ds(pl.multiple_of(index * LANES, LANES), LANES)
            a[part, cols] = attend(q[part, cols], k[part, cols], v[part, cols], same[few])
            return carry

        lax.fori_loop(0, width // LANES, time_pair, 0, unroll=UNROLL_T)
        if c == 0:
            waits[3]()
        after = (tok.astype(F32) + project(a[part], weights[3][...])).astype(BF16)
        after = jnp.concatenate([after[:, n * columns : (n + 1) * columns] for n in range(fold)], 0)
        if fold > 1:
            after = project(folding[few], after)
        snd[c][...] = after.astype(F32).reshape(frames, piece, columns).astype(BF16)
        send(c, 0, straight)
        pltpu.make_async_remote_copy(
            src_ref=snd[c].at[(me_t * chips + me_z) * 2 + 1 - me_c],
            dst_ref=rcv[c].at[me_s * slots + me_t],
            send_sem=s2.at[c],
            recv_sem=r2.at[c],
            device_id={"space": me_z * 2 + 1 - me_c},
        ).start()
        send(c, 1, everyone[: EARLY[c]])
        rcv[c][me_s * slots + me_t] = snd[c][me_t * rows + me_s]
    for c in range(count):
        send(c, 1, everyone[EARLY[c] :])

    for h in range(halves):
        mine = [(c, first_place, few) for c, (own, first_place, few) in enumerate(chunks) if own == h]
        for c, _, _ in mine:
            second_all(c).wait_recv()
        arrived = [(flat(rcv[c][...]), first_place, few) for c, first_place, few in mine]
        finest = max(piece // few for _, _, few in arrived)
        columns = width // finest
        parts = []
        for n in range(finest):
            def source(r):
                place, found = r % piece, r
                for m, (_, first_place, few) in enumerate(arrived):
                    part = n * piece // (finest * few)
                    row = m * tokens + (r // piece) * piece + part * few + place - first_place
                    found = jnp.where(place >= first_place, row, found)
                return found

            stack = []
            for block, _, few in arrived:
                start = (n % (finest * few // piece)) * columns
                stack.append(block[:, start : start + columns])
            hot = one_hot((tokens, len(arrived) * tokens), source)
            parts.append(project(hot, jnp.concatenate(stack, 0)).astype(BF16))
        frame = jnp.concatenate(parts, 1)
        res[:, :, h] = frame.astype(F32).reshape(spread, slots, piece, width).astype(BF16)
        qkv(
            layer_norm(frame, sg[...], ss[...]),
            weights[4:7],
            waits[4:7] if h == 0 else [lambda: None] * 3,
            [ref.at[pl.ds(h * tokens, tokens)] for ref in (q, k, v)],
        )
    waits[7]()
    share = slots * piece
    both = 2 * share

    def third(target):
        return pltpu.make_async_remote_copy(
            src_ref=res.at[target],
            dst_ref=out.at[me_s],
            send_sem=s3,
            recv_sem=r3,
            device_id={"space": target},
        )

    near = chips // 2
    targets = [(1 - me_z // near) * near + n for n in range(near)] if near else []
    targets += [moved(me_z, steps_z, mask) for mask in range(near - 1, 0, -1)]
    for target in targets + [me_z]:
        parts = [
            pl.ds(pl.multiple_of(h * tokens + target * both, both), both) for h in range(halves)
        ]

        def attend_pair(index, carry):
            cols = pl.ds(pl.multiple_of(index * LANES, LANES), LANES)
            queries = jnp.concatenate([q[part, cols] for part in parts], 0)
            result = attend(queries, k[:, cols], v[:, cols], None)
            for h, part in enumerate(parts):
                a[part, cols] = result[h * both : (h + 1) * both]
            return carry

        lax.fori_loop(0, width // LANES, attend_pair, 0, unroll=UNROLL_S)
        added = project(jnp.concatenate([a[part] for part in parts], 0), weights[7][...])
        here = pl.ds(2 * target, 2)
        for h in range(halves):
            new = added[h * both : (h + 1) * both].reshape(2, slots, piece, width)
            res[here, :, h] = (res[here, :, h].astype(F32) + new).astype(BF16)
        if target is me_z:
            third(me_s + 1 - 2 * me_c).start()
        else:
            for core in (1, 0):
                third(2 * target + core).start()
    last = pltpu.make_async_copy(res.at[me_s], out.at[me_s], lsem.at[0])
    last.start()
    for c in range(count):
        first_all(c).wait_send()
        second_all(c).wait_send()
    others = pl.ds(0, spread - 1)
    pltpu.make_async_remote_copy(
        src_ref=res.at[others],
        dst_ref=out.at[others],
        send_sem=s3,
        recv_sem=r3,
        device_id={"space": me_s + 1 - 2 * me_c},
    ).wait()
    last.wait()


def run_layer(frames_in, slots, spread, norms, weights):
    rows, patches, width = frames_in.shape
    frames, places, halves = rows * slots, patches // slots, 2
    piece = places // halves
    total = frames * places
    fews = [few for plan in PLAN for few in plan]
    vmem, hbm = pl.BlockSpec(memory_space=pltpu.VMEM), pl.BlockSpec(memory_space=pltpu.HBM)
    dma = pltpu.SemaphoreType.DMA
    return pl.pallas_call(
        functools.partial(layer_kernel, slots, spread),
        out_shape=pltpu.VMEM((rows, slots, halves, piece, width), BF16),
        in_specs=[hbm] * 13,
        out_specs=vmem,
        scratch_shapes=[
            pltpu.VMEM((4, 1, width), F32),
            pltpu.VMEM((8, width, width), BF16),
            pltpu.VMEM((halves, rows, slots, piece, width), BF16),
            pltpu.VMEM((spread, slots, halves, piece, width), BF16),
        ]
        + [pltpu.VMEM((total, width), BF16)] * 4
        + [
            dma((4,)),
            dma((8,)),
            dma((halves,)),
            dma((len(fews),)),
            dma((len(fews),)),
            dma((len(fews),)),
            dma((len(fews),)),
            dma(()),
            dma(()),
        ]
        + [pltpu.VMEM((slots, rows * few, width), BF16) for few in fews]
        + [pltpu.VMEM((frames * few, width), BF16) for few in fews]
        + [pltpu.VMEM((frames, piece, width * few // piece), BF16) for few in fews]
        + [pltpu.VMEM((slots * spread, piece, width * few // piece), BF16) for few in fews],
        compiler_params=pltpu.CompilerParams(
            collective_id=0, has_side_effects=True, vmem_limit_bytes=60 << 20
        ),
    )(
        frames_in.reshape(rows, slots, halves, piece, width),
        *[norm.reshape(1, -1) for norm in norms],
        *weights,
    ).reshape(frames_in.shape)


def split_heads(tokens):
    return tokens.reshape(tokens.shape[0], tokens.shape[1], tokens.shape[2] // HEAD_DIM, HEAD_DIM)


def gathered_space(after_time, gain, shift, wq, wk, wv, wo):
    normed = layer_norm(after_time, gain, shift)
    queries = project(normed, wq).astype(BF16)
    everywhere = lax.all_gather(normed, "space", axis=1, tiled=True)
    keys_in, values_in = (project(everywhere, w).astype(BF16) for w in (wk, wv))
    scores = 0.125 * jnp.einsum(
        "fqhd,fkhd->fhqk", split_heads(queries), split_heads(keys_in), preferred_element_type=F32
    )
    weights = jax.nn.softmax(scores, axis=-1).astype(BF16)
    spatial = jnp.einsum(
        "fhqk,fkhd->fqhd", weights, split_heads(values_in), preferred_element_type=F32
    )
    spatial = spatial.astype(BF16).reshape(after_time.shape)
    return (after_time.astype(F32) + project(spatial, wo)).astype(BF16)


def body(frames_in, tg, ts, tq, tk, tv, to, sg, ss, sq, sk, sv, so):
    slots, spread = lax.axis_size("tm"), lax.axis_size("space")
    rows, patches, width = frames_in.shape
    frames, places = rows * slots, patches // slots
    powers = not (slots & (slots - 1) or spread & (spread - 1)) and spread % 2 == 0
    tiles = places == 16 and width % (4 * LANES) == 0
    if rows == spread and powers and tiles:
        return run_layer(
            frames_in, slots, spread, (tg, ts, sg, ss), (tq, tk, tv, to, sq, sk, sv, so)
        )
    tokens = lax.all_to_all(
        frames_in.reshape(rows, slots, places, width), "tm", split_axis=1, concat_axis=0, tiled=True
    ).reshape(frames * places, width)
    after = run_branch(functools.partial(time_branch, frames), tokens, tg, ts, tq, tk, tv, to)
    after = lax.all_to_all(
        after.reshape(frames, 1, places, width), "tm", split_axis=0, concat_axis=1, tiled=True
    ).reshape(rows, patches, width)
    return gathered_space(after, sg, ss, sq, sk, sv, so)


def solution(mesh):
    return jax.shard_map(
        body,
        mesh=mesh,
        in_specs=(P("tm", "space", None),) + (P(),) * 12,
        out_specs=P("tm", "space", None),
        check_vma=False,
    )
```
